32 devices in a mesh: fsdp: 8 (over y, x, core), seq: 4 (over z).
Axes of the slice: x: 2, y: 2, z: 4, core: 2. Of those that a mesh axis runs over, the one named last changes fastest.
Arguments:
- inputs: bfloat16 [3, 8, 1024, 1024], P(None, 'fsdp', 'seq'), may hold values from -6 to 6
- segment_ids: int32 [3, 8, 1024], P(None, 'fsdp'), may hold values from 0 to 3, never falling along the last dimension, each value on 1 to 512 neighbouring positions
- buckets: int32 [1024], replicated, may hold values from 0 to 31, as said below
- ln1_gain: bfloat16 [1024], P('fsdp'), may hold values from 0.5 to 1.5
- ln1_bias: bfloat16 [1024], P('fsdp'), may hold values from -3 to 3
- w_query: bfloat16 [1024, 1024], P('fsdp'), may hold values from -0.1875 to 0.1875
- w_key: bfloat16 [1024, 1024], P('fsdp'), may hold values from -0.1875 to 0.1875
- w_value: bfloat16 [1024, 1024], P('fsdp'), may hold values from -0.1875 to 0.1875
- w_out: bfloat16 [1024, 1024], P('fsdp'), may hold values from -0.75 to 0.75
- rel_bias: bfloat16 [32, 16], P('fsdp'), may hold values from -4 to 4
- second_norm_gain: bfloat16 [1024], P('fsdp'), may hold values from 0.5 to 1.5
- ln2_bias: bfloat16 [1024], P('fsdp'), may hold values from -3 to 3
- w_up: bfloat16 [1024, 4096], P('fsdp'), may hold values from -0.1875 to 0.1875
- b_up: bfloat16 [4096], P('fsdp'), may hold values from -3 to 3
- w_down: bfloat16 [4096, 1024], P('fsdp'), may hold values from -0.09375 to 0.09375
- b_down: bfloat16 [1024], P('fsdp'), may hold values from -3 to 3
- cotangent: bfloat16 [3, 8, 1024, 1024], P(None, 'fsdp', 'seq'), may hold values from -6 to 6
Outputs:
- outputs: bfloat16 [3, 8, 1024, 1024], P(None, 'fsdp', 'seq')
- input_grad: bfloat16 [3, 8, 1024, 1024], P(None, 'fsdp', 'seq')
- grad_ln1_gain: float32 [1024], P('fsdp')
- grad_ln1_bias: float32 [1024], P('fsdp')
- grad_w_query: float32 [1024, 1024], P('fsdp')
- grad_w_key: float32 [1024, 1024], P('fsdp')
- grad_w_value: float32 [1024, 1024], P('fsdp')
- grad_w_out: float32 [1024, 1024], P('fsdp')
- grad_rel_bias: float32 [32, 16], P('fsdp')
- grad_ln2_gain: float32 [1024], P('fsdp')
- grad_ln2_bias: float32 [1024], P('fsdp')
- grad_w_up: float32 [1024, 4096], P('fsdp')
- grad_b_up: float32 [4096], P('fsdp')
- grad_w_down: float32 [4096, 1024], P('fsdp')
- grad_b_down: float32 [1024], P('fsdp')
The draws below stay inside these ranges and needn't reach their ends.
Inputs may be any that keep to these rules, and one draw needn't show every extreme that they name: `segment_ids`: along a row the clip number never falls; each clip of a row has 1 to 512 tokens, and some clip has exactly 512. `buckets`: the bucket never falls as the distance grows; it is 0 at distance 0 and 31 at distance 1024 - 1.
All inputs are finite; a program needn't handle non-finite values.
Results may differ from the reference program's by a relative error of at most 0.025.
Values may be sent and summed in bfloat16 or wider, within the bound.
No kernel may reach another device: no remote copies, remote signals or barrier semaphores. Data moves between devices by JAX's collectives and lax.ppermute only.
A program may use at most 448 MiB of HBM per device.

```python
import math
import jax
import jax.numpy as jnp
import numpy as np
from jax import lax

D = 1024
HEADS = 16
HEAD_DIM = 64
FF = 4096
BUCKETS = 32
MICRO = 3
CLIPS = 4
SEQLEN = 1024
ROWS = 8


def draw_buckets(key, part):
    increments = jax.random.randint(key, (SEQLEN,), 0, 2, dtype=jnp.int32)
    increments = increments.at[0].set(0).at[1].set(1)
    climbing = jnp.cumsum(increments).astype(jnp.int32)
    return (climbing * (BUCKETS - 1) // climbing[-1]).astype(jnp.int32)


def shard_levels(rng, extent, shards, smallest, high):
    def one(position, parts):
        heights = jax.random.uniform(jax.random.fold_in(jax.random.fold_in(rng, 6), position), (parts,), jnp.float32, smallest / len(shards), high / len(shards))
        return jnp.repeat(jnp.exp(heights), extent[position] // parts).reshape((-1,) + (1,) * (len(extent) - position - 1))

    gain = one(*shards[0])
    for cut in shards[1:]:
        gain = gain * one(*cut)
    return gain


def length_profile(number_of, total, limit, slope):
    loads = [(1 << 20) // math.isqrt(rank ** slope) + 1 for rank in range(2, number_of + 1)]
    spare, holding = total - limit - (number_of - 1), [1] * (number_of - 1)
    while spare > 0:
        free = [i for i in range(number_of - 1) if holding[i] < limit]
        pool, remaining = sum([loads[i] for i in free]), spare
        for i in free:
            more = min(limit - holding[i], max(1, remaining * loads[i] // pool), spare)
            holding[i] = holding[i] + more
            spare = spare - more
    return np.array([limit] + holding)


def uneven(own_key, number_of, total, reach, lean):
    if number_of == 2:
        one = jax.random.randint(own_key, (), max(1, total - reach), min(reach, total - 1) + 1)
        return jnp.stack([one, total - one])
    sizes = jnp.asarray(length_profile(number_of, total, reach, lean), jnp.int32)
    twos = (number_of - 1) // 2
    giver, taker = sizes[1:1 + 2 * twos:2], sizes[2:2 + 2 * twos:2]
    room = jnp.minimum(giver - 1, reach - taker)
    passed = jax.random.randint(jax.random.fold_in(own_key, 1), (twos,), 0, 1 << 20) % (room + 1)
    sizes = sizes.at[1:1 + 2 * twos:2].set(giver - passed).at[2:2 + 2 * twos:2].set(taker + passed)
    return sizes[jax.random.permutation(jax.random.fold_in(own_key, 2), number_of)]


def normal_values(key, dims, width, limit, pieces=(), kind=jnp.bfloat16):
    drawn = jax.random.normal(key, dims, jnp.float32) * width
    if len(pieces) > 0:
        drawn = shard_levels(key, dims, pieces, -0.22, 0.18) * drawn
    return jnp.clip(drawn, min=-limit, max=limit).astype(kind)


def setup_inputs(seed: int = 0) -> dict:
    key_list = jax.random.split(jax.random.key(seed), 18)
    inputs = normal_values(key_list[0], (MICRO, ROWS, SEQLEN, D), 1.0, 6.0, ((1, 8), (2, 4)))
    segment_ids = jax.vmap(lambda own: jnp.searchsorted(jnp.cumsum(uneven(own, CLIPS, SEQLEN, SEQLEN // 2, 0)), jnp.arange(SEQLEN), side="right"))(jax.random.split(key_list[1], MICRO * ROWS)).reshape((MICRO, ROWS, SEQLEN)).astype(jnp.int32)
    buckets = draw_buckets(jax.random.fold_in(key_list[17], 71), 0)
    ln1_gain = jnp.clip(1.0 + 0.1 * jax.random.normal(key_list[3], (D,), jnp.float32), 0.5, 1.5).astype(jnp.bfloat16)
    ln1_bias = normal_values(key_list[4], (D,), 0.5, 3.0, ((0, 8),))
    w_query = normal_values(key_list[5], (D, D), D ** -0.5, 0.1875, ((0, 8),))
    w_key = normal_values(key_list[6], (D, D), D ** -0.5, 0.1875, ((0, 8),))
    w_value = normal_values(key_list[7], (D, D), D ** -0.5, 0.1875, ((0, 8),))
    w_out = normal_values(key_list[8], (D, D), (D // 16) ** -0.5, 0.75, ((0, 8),))
    rel_bias = normal_values(key_list[9], (BUCKETS, HEADS), 1.0, 4.0, ((0, 8),))
    second_norm_gain = jnp.clip(1.0 + 0.1 * jax.random.normal(key_list[10], (D,), jnp.float32), 0.5, 1.5).astype(jnp.bfloat16)
    ln2_bias = normal_values(key_list[11], (D,), 0.5, 3.0, ((0, 8),))
    w_up = normal_values(key_list[12], (D, FF), D ** -0.5, 0.1875, ((0, 8),))
    b_up = normal_values(key_list[13], (FF,), 0.5, 3.0, ((0, 8),))
    w_down = normal_values(key_list[14], (FF, D), FF ** -0.5, 0.09375, ((0, 8),))
    b_down = normal_values(key_list[15], (D,), 0.5, 3.0, ((0, 8),))
    cotangent = normal_values(key_list[16], (MICRO, ROWS, SEQLEN, D), 1.0, 6.0, ((1, 8), (2, 4)))
    return {"inputs": inputs, "segment_ids": segment_ids, "buckets": buckets, "ln1_gain": ln1_gain, "ln1_bias": ln1_bias, "w_query": w_query, "w_key": w_key, "w_value": w_value, "w_out": w_out, "rel_bias": rel_bias, "second_norm_gain": second_norm_gain, "ln2_bias": ln2_bias, "w_up": w_up, "b_up": b_up, "w_down": w_down, "b_down": b_down, "cotangent": cotangent}


epsilon = 1e-05
masked_out = -1e+30
EXACT_PRECISION = lax.Precision.HIGHEST

@jax.custom_vjp
def low(v):
    return lax.optimization_barrier(v.astype(jnp.bfloat16)).astype(jnp.float32)

@jax.custom_vjp
def low_back(v):
    return v

def low_keep(v):
    return (low(v), None)

def low_pass(kept, grad):
    return (grad,)

def back_keep(v):
    return (v, None)

def back_low(kept, grad):
    return (low(grad),)
low.defvjp(low_keep, low_pass)
low_back.defvjp(back_keep, back_low)

def layer_norm(field, norm_gain, norm_shift):
    centre = field - lax.optimization_barrier(jnp.mean(field, axis=-1, keepdims=True))
    spread = lax.optimization_barrier(jnp.mean(centre * centre, axis=-1, keepdims=True))
    return centre * lax.rsqrt(spread + epsilon) * norm_gain + norm_shift

def forward_row(row_x, params, seg_mask, bucket_mat):
    norm1_gain, norm1_shift, query_mat, key_mat, value_mat, out_mat, rel_table, norm2_gain, norm2_shift, up_mat, up_bias, down_mat, down_bias = params
    seq_len = row_x.shape[0]
    normed_one = low(layer_norm(row_x, norm1_gain, norm1_shift))
    queries = low_back(low(jnp.dot(normed_one, query_mat, precision=EXACT_PRECISION)))
    keys_row = low_back(low(jnp.dot(normed_one, key_mat, precision=EXACT_PRECISION)))
    values_row = low_back(low(jnp.dot(normed_one, value_mat, precision=EXACT_PRECISION)))
    query_three = queries.reshape(seq_len, HEADS, HEAD_DIM)
    key_three = keys_row.reshape(seq_len, HEADS, HEAD_DIM)
    value_three = values_row.reshape(seq_len, HEADS, HEAD_DIM)
    score_position_bias = jnp.transpose(rel_table[bucket_mat], (2, 0, 1))
    raw_scores = jnp.einsum('qhd,khd->hqk', query_three, key_three, precision=EXACT_PRECISION) * HEAD_DIM ** (-0.5) + score_position_bias
    raw_scores = low_back(raw_scores)
    logits = jnp.where(seg_mask[None], raw_scores, masked_out)
    soft_probs = low(jax.nn.softmax(logits, axis=-1))
    attended = jnp.einsum('hqk,khd->qhd', soft_probs, value_three, precision=EXACT_PRECISION).reshape(seq_len, D)
    attended = low_back(low(attended))
    middle = row_x + low_back(jnp.dot(attended, out_mat, precision=EXACT_PRECISION))
    normed_two = low(layer_norm(middle, norm2_gain, norm2_shift))
    pre_act = low_back(jnp.dot(normed_two, up_mat, precision=EXACT_PRECISION) + up_bias)
    activation = low(jax.nn.gelu(pre_act, approximate=False))
    return middle + jnp.dot(activation, down_mat, precision=EXACT_PRECISION) + down_bias

def reference(inputs, segment_ids, buckets, ln1_gain, ln1_bias, w_query, w_key, w_value, w_out, rel_bias, second_norm_gain, ln2_bias, w_up, b_up, w_down, b_down, cotangent):
    params = tuple((weight.astype(jnp.float32) for weight in (ln1_gain, ln1_bias, w_query, w_key, w_value, w_out, rel_bias, second_norm_gain, ln2_bias, w_up, b_up, w_down, b_down)))
    positions = jnp.arange(SEQLEN, dtype=jnp.int32)
    distance = positions[:, None] - positions[None, :]
    causal = distance >= 0
    bucket_mat = buckets[jnp.maximum(distance, 0)].astype(jnp.int32)
    flat_x = inputs.reshape(MICRO * ROWS, SEQLEN, D)
    flat_segs = segment_ids.reshape(MICRO * ROWS, SEQLEN)
    flat_cot = cotangent.reshape(MICRO * ROWS, SEQLEN, D)

    def row_step(totals, record):
        row_x, row_seg, row_cot = record
        seg_mask = causal & (row_seg[:, None] == row_seg[None, :])

        def forward_one(field, weights_all):
            return forward_row(field, weights_all, seg_mask, bucket_mat)
        result_row, pull_back = jax.vjp(forward_one, row_x.astype(jnp.float32), params)
        grad_row, grad_params = pull_back(row_cot.astype(jnp.float32))
        totals = jax.tree.map(jnp.add, totals, grad_params)
        return (totals, (result_row.astype(jnp.bfloat16), grad_row.astype(jnp.bfloat16)))
    starting = tuple((jnp.zeros(weight.shape, jnp.float32) for weight in params))
    totals, (result_rows, grad_rows) = lax.scan(row_step, starting, (flat_x, flat_segs, flat_cot))
    outputs = result_rows.reshape(MICRO, ROWS, SEQLEN, D)
    input_grad = grad_rows.reshape(MICRO, ROWS, SEQLEN, D)
    return (outputs, input_grad, totals[0], totals[1], totals[2], totals[3], totals[4], totals[5], totals[6], totals[7], totals[8], totals[9], totals[10], totals[11], totals[12])
```

```python
import functools

import jax
import jax.numpy as jnp
from jax import lax
from jax.experimental import pallas as pl
from jax.experimental.pallas import tpu as pltpu
from jax.sharding import PartitionSpec as P

EPS = 1e-05
NEG = -1e30
CLIP = 512
F32 = jnp.float32
BF16 = jnp.bfloat16
HIGHEST = lax.Precision.HIGHEST
MIB = 1 << 20

ERFC_P = 0.4375
ERFC_C = (
    0.24679607152938843,
    0.24772192537784576,
    0.2143726497888565,
    0.22321343421936035,
    -0.03611995279788971,
    0.3185710310935974,
    -0.2865786552429199,
    0.07202363014221191,
)


def params(vmem=56):
    return pltpu.CompilerParams(vmem_limit_bytes=vmem * MIB)


def cost(flops, nbytes, trans=0):
    return pl.CostEstimate(flops=int(flops), bytes_accessed=int(nbytes), transcendentals=int(trans))


def gelu_parts(u):
    tail = jnp.exp(u * u * -0.5)
    t = 1.0 / (1.0 + jnp.abs(u) * (ERFC_P * 0.5**0.5))
    poly = jnp.full_like(u, 0.5 * ERFC_C[-1])
    for c in ERFC_C[-2::-1]:
        poly = poly * t + 0.5 * c
    half = poly * t * tail
    cdf = jnp.where(u >= 0, 1.0 - half, half)
    return u * cdf, cdf + u * tail * 0.3989422804014327


def dot_nn(a, b):
    return lax.dot_general(a, b, (((1,), (0,)), ((), ())), preferred_element_type=F32)


def dot_nt(a, b):
    return lax.dot_general(a, b, (((1,), (1,)), ((), ())), preferred_element_type=F32)


def dot_tn(a, b):
    return lax.dot_general(a, b, (((0,), (0,)), ((), ())), preferred_element_type=F32)


def bias_kernel(qb, row_ref, out_ref):
    width = row_ref.shape[-1]
    block = jnp.broadcast_to(row_ref[0], (8, width))
    sub = lax.broadcasted_iota(jnp.int32, (8, width), 0)
    for bit in range(3):
        block = jnp.where((sub >> bit) & 1 == 1, pltpu.roll(block, 1 << bit, 1), block)
    rows = 8
    while rows < qb:
        block = jnp.concatenate([block, pltpu.roll(block, rows, 1)], axis=0)
        rows *= 2
    out_ref[0] = block[:, : out_ref.shape[-1]]


def make_bias(row, qb, kw):
    heads, width = row.shape
    return pl.pallas_call(
        functools.partial(bias_kernel, qb),
        grid=(heads,),
        in_specs=[pl.BlockSpec((1, 1, width), lambda h: (h, 0, 0))],
        out_specs=pl.BlockSpec((1, qb, kw), lambda h: (h, 0, 0)),
        out_shape=jax.ShapeDtypeStruct((heads, qb, kw), F32),
        compiler_params=params(),
        cost_estimate=cost(0, heads * qb * kw * 4),
        name="bias_table",
    )(row[:, None, :])


def diagonal_sums(block, width):
    qb, kw = block.shape
    if width > kw:
        block = jnp.concatenate([block, jnp.zeros((qb, width - kw), F32)], axis=1)
    rows = qb
    while rows > 8:
        rows //= 2
        block = block[:rows] + pltpu.roll(block[rows:], width - rows, 1)
    sub = lax.broadcasted_iota(jnp.int32, (8, width), 0)
    for bit in range(3):
        block = jnp.where((sub >> bit) & 1 == 1, pltpu.roll(block, width - (1 << bit), 1), block)
    return jnp.sum(block, axis=0, keepdims=True)


def norm_kernel(hops, *refs):
    gain = refs[hops + 1][...]
    shift = refs[hops + 2][...]
    out_ref = refs[hops + 3]
    size = refs[0].shape[1]
    for b in range(hops + 1):
        field = refs[b][0].astype(F32)
        centre = field - jnp.mean(field, axis=-1, keepdims=True)
        spread = jnp.mean(centre * centre, axis=-1, keepdims=True)
        out_ref[0, b * size : (b + 1) * size] = (centre * lax.rsqrt(spread + EPS) * gain + shift).astype(BF16)


def norm_window(blocks, gain, shift):
    rows, size, width = blocks[0].shape
    n = len(blocks)
    return pl.pallas_call(
        functools.partial(norm_kernel, n - 1),
        grid=(rows,),
        in_specs=[pl.BlockSpec((1, size, width), lambda r: (r, 0, 0))] * n
        + [pl.BlockSpec((1, width), lambda r: (0, 0))] * 2,
        out_specs=pl.BlockSpec((1, n * size, width), lambda r: (r, 0, 0)),
        out_shape=jax.ShapeDtypeStruct((rows, n * size, width), BF16),
        compiler_params=params(),
        cost_estimate=cost(10 * rows * n * size * width, rows * n * size * width * 4),
        name="norm_window",
    )(*blocks, gain, shift)


def proj_kernel(scale, x_ref, w_ref, o_ref):
    out = dot_nn(x_ref[...], w_ref[...]).astype(BF16)
    o_ref[...] = out * scale if scale != 1.0 else out


def project(x, w, block_rows, row_step, row_first, col_first, cols, bn, scale, name):
    depth = x.shape[1]
    count = x.shape[0] // (block_rows * row_step)
    return pl.pallas_call(
        functools.partial(proj_kernel, scale),
        grid=(cols // bn, count),
        in_specs=[
            pl.BlockSpec((block_rows, depth), lambda n, r: (r * row_step + row_first, 0)),
            pl.BlockSpec((depth, bn), lambda n, r: (0, n + col_first // bn)),
        ],
        out_specs=pl.BlockSpec((block_rows, bn), lambda n, r: (r, n)),
        out_shape=jax.ShapeDtypeStruct((count * block_rows, cols), BF16),
        compiler_params=params(),
        cost_estimate=cost(2 * count * block_rows * depth * cols, 2 * (x.size + depth * cols + count * block_rows * cols)),
        name=name,
    )(x, w)


def split_pair(field, even):
    zero = jnp.zeros_like(field)
    return jnp.concatenate([jnp.where(even, field, zero), jnp.where(even, zero, field)], axis=0)


def join_pair(field, even):
    half = field.shape[0] // 2
    return jnp.where(even, field[:half], field[half:])


def attn_fwd_kernel(qb, q_ref, k_ref, v_ref, bias_ref, mask_ref, o_ref, inv_ref, e_ref):
    blocks = q_ref.shape[0] // qb
    kw = bias_ref.shape[-1]
    even = lax.broadcasted_iota(jnp.int32, (qb, 128), 1) < 64
    for b in range(blocks):
        rows = slice(b * qb, (b + 1) * qb)
        keys = slice(b * qb, b * qb + kw)
        scores = dot_nt(split_pair(q_ref[rows], even), k_ref[keys])
        mask = mask_ref[0, b]
        scores = jnp.concatenate(
            [scores[:qb] + (bias_ref[0] + mask), scores[qb:] + (bias_ref[1] + mask)], axis=0
        )
        peak = jnp.max(scores, axis=-1, keepdims=True)
        expo = jnp.exp(scores - peak)
        inv = 1.0 / jnp.sum(expo, axis=-1, keepdims=True)
        expo = expo.astype(BF16)
        e_ref[0, 0, b] = expo
        inv = join_pair(jnp.broadcast_to(inv, (2 * qb, 128)), even)
        mixed = join_pair(dot_nn(expo, v_ref[keys]), even)
        inv_ref[rows] = inv
        o_ref[rows] = (mixed * inv).astype(BF16)


def attn_fwd(q, kv, bias, mask):
    heads, qb, kw = bias.shape
    pairs = heads // 2
    rows, blocks = mask.shape[:2]
    size = blocks * qb
    window = kv.shape[0] // rows
    cells = rows * blocks * heads * qb * kw
    return pl.pallas_call(
        functools.partial(attn_fwd_kernel, qb),
        grid=(rows, pairs),
        in_specs=[
            pl.BlockSpec((size, 128), lambda r, p: (r, p)),
            pl.BlockSpec((window, 128), lambda r, p: (r, p)),
            pl.BlockSpec((window, 128), lambda r, p: (r, p + pairs)),
            pl.BlockSpec((2, qb, kw), lambda r, p: (p, 0, 0)),
            pl.BlockSpec((1, blocks, qb, kw), lambda r, p: (r, 0, 0, 0)),
        ],
        out_specs=[
            pl.BlockSpec((size, 128), lambda r, p: (r, p)),
            pl.BlockSpec((size, 128), lambda r, p: (r, p)),
            pl.BlockSpec((1, 1, blocks, 2 * qb, kw), lambda r, p: (r, p, 0, 0, 0)),
        ],
        out_shape=[
            jax.ShapeDtypeStruct(q.shape, BF16),
            jax.ShapeDtypeStruct(q.shape, F32),
            jax.ShapeDtypeStruct((rows, pairs, blocks, 2 * qb, kw), BF16),
        ],
        compiler_params=params(),
        cost_estimate=cost(cells * 256, cells * 4, cells),
        name="attn_fwd",
    )(q, kv, kv, bias, mask)


def attn_bwd_kernel(qb, width, q_ref, k_ref, v_ref, e_ref, inv_ref, o_ref, g_ref, dq_ref, dk_ref, dv_ref, diag_ref, sums, dk_acc, dv_acc):
    blocks = q_ref.shape[0] // qb
    kw = e_ref.shape[-1]
    row, pair = pl.program_id(0), pl.program_id(1)
    even = lax.broadcasted_iota(jnp.int32, (qb, 128), 1) < 64
    dk_acc[...] = jnp.zeros_like(dk_acc)
    dv_acc[...] = jnp.zeros_like(dv_acc)

    @pl.when(row == 0)
    def _():
        sums[pair] = jnp.zeros(sums.shape[1:], F32)

    for b in range(blocks):
        rows = slice(b * qb, (b + 1) * qb)
        keys = slice(b * qb, b * qb + kw)
        grad = (g_ref[rows].astype(F32) * inv_ref[rows]).astype(BF16)
        weigh = grad.astype(F32) * o_ref[rows].astype(F32)
        delta = jnp.sum(split_pair(weigh, even), axis=-1, keepdims=True)
        grad = split_pair(grad, even)
        expo = e_ref[0, 0, b]
        dscore = expo.astype(F32) * (dot_nt(grad, v_ref[keys]) - delta)
        sums[pair] += dscore
        dscore = dscore.astype(BF16)
        dq_ref[rows] = (join_pair(dot_nn(dscore, k_ref[keys]), even) * 0.125).astype(BF16)
        dk_acc[:, keys] += dot_tn(split_pair(q_ref[rows], even), dscore)
        dv_acc[:, keys] += dot_tn(grad, expo)

    dk_ref[0] = dk_acc[...].astype(BF16)
    dv_ref[0] = dv_acc[...].astype(BF16)

    @pl.when(row == pl.num_programs(0) - 1)
    def _():
        diag_ref[0, 0:1] = diagonal_sums(sums[pair, :qb], width)
        diag_ref[0, 1:2] = diagonal_sums(sums[pair, qb:], width)


def attn_bwd(q, kv, e, inv, o, g, width):
    rows, pairs, blocks, qb2, kw = e.shape
    qb = qb2 // 2
    size = blocks * qb
    window = kv.shape[0] // rows
    model = q.shape[1]
    cells = e.size
    return pl.pallas_call(
        functools.partial(attn_bwd_kernel, qb, width),
        grid=(rows, pairs),
        in_specs=[
            pl.BlockSpec((size, 128), lambda r, p: (r, p)),
            pl.BlockSpec((window, 128), lambda r, p: (r, p)),
            pl.BlockSpec((window, 128), lambda r, p: (r, p + pairs)),
            pl.BlockSpec((1, 1, blocks, qb2, kw), lambda r, p: (r, p, 0, 0, 0)),
            pl.BlockSpec((size, 128), lambda r, p: (r, p)),
            pl.BlockSpec((size, 128), lambda r, p: (r, p)),
            pl.BlockSpec((size, 128), lambda r, p: (r, p)),
        ],
        out_specs=[
            pl.BlockSpec((size, 128), lambda r, p: (r, p)),
            pl.BlockSpec((1, 128, window), lambda r, p: (r, p, 0)),
            pl.BlockSpec((1, 128, window), lambda r, p: (r, p, 0)),
            pl.BlockSpec((1, 8, width), lambda r, p: (p, 0, 0)),
        ],
        out_shape=[
            jax.ShapeDtypeStruct(q.shape, BF16),
            jax.ShapeDtypeStruct((rows, model, window), BF16),
            jax.ShapeDtypeStruct((rows, model, window), BF16),
            jax.ShapeDtypeStruct((pairs, 8, width), F32),
        ],
        scratch_shapes=[pltpu.VMEM((pairs, qb2, kw), F32)] + [pltpu.VMEM((128, window), F32)] * 2,
        compiler_params=params(),
        cost_estimate=cost(cells * 512, cells * 4),
        name="attn_bwd",
    )(q, kv, kv, e, inv, o, g)


def middle_kernel(a_ref, w_ref, x_ref, gain_ref, shift_ref, mid_ref, norm_ref):
    middle = x_ref[...].astype(F32) + dot_nn(a_ref[...], w_ref[...])
    mid_ref[...] = middle
    centre = middle - jnp.mean(middle, axis=-1, keepdims=True)
    spread = jnp.mean(centre * centre, axis=-1, keepdims=True)
    norm_ref[...] = (centre * lax.rsqrt(spread + EPS) * gain_ref[...] + shift_ref[...]).astype(BF16)


def middle_block(attended, w_out, x, gain, shift, bm):
    tokens, model = x.shape
    tile = pl.BlockSpec((bm, model), lambda i: (i, 0))
    line = pl.BlockSpec((1, model), lambda i: (0, 0))
    return pl.pallas_call(
        middle_kernel,
        grid=(tokens // bm,),
        in_specs=[tile, pl.BlockSpec((model, model), lambda i: (0, 0)), tile, line, line],
        out_specs=[tile, tile],
        out_shape=[jax.ShapeDtypeStruct((tokens, model), F32), jax.ShapeDtypeStruct((tokens, model), BF16)],
        compiler_params=params(),
        cost_estimate=cost(2 * tokens * model * model, tokens * model * 10 + model * model * 2),
        name="middle_block",
    )(attended, w_out, x, gain, shift)


def ffn_kernel(bm, n2_ref, cot_ref, wu_ref, bu_ref, wd_ref, out_ref, gn_ref, gwu_ref, gwd_ref, gbu_ref, act_s, gpre_s):
    step = pl.program_id(0)
    tokens = n2_ref.shape[0]

    @pl.when(step == 0)
    def _():
        out_ref[...] = jnp.zeros_like(out_ref)
        gn_ref[...] = jnp.zeros_like(gn_ref)

    gbu_ref[...] = jnp.zeros_like(gbu_ref)

    @pl.loop(0, tokens // bm)
    def _(i):
        rows = pl.ds(pl.multiple_of(i * bm, bm), bm)
        act, slope = gelu_parts(dot_nn(n2_ref[rows, :], wu_ref[...]) + bu_ref[...])
        gpre = (dot_nt(cot_ref[rows, :], wd_ref[...]) * slope).astype(BF16)
        act = act.astype(BF16)
        act_s[rows, :] = act
        gpre_s[rows, :] = gpre
        gbu_ref[...] += jnp.sum(gpre.astype(F32), axis=0, keepdims=True)
        out_ref[rows, :] += dot_nn(act, wd_ref[...])
        gn_ref[rows, :] += dot_nt(gpre, wu_ref[...])

    gwd_ref[...] = dot_tn(act_s[...], cot_ref[...]).astype(BF16)
    gwu_ref[...] = dot_tn(n2_ref[...], gpre_s[...]).astype(BF16)


def ffn_block(n2, cot, w_up, b_up, w_down, fc, bm):
    tokens, model = n2.shape
    hidden = w_up.shape[1]
    whole = pl.BlockSpec((tokens, model), lambda j: (0, 0))
    return pl.pallas_call(
        functools.partial(ffn_kernel, bm),
        grid=(hidden // fc,),
        in_specs=[
            whole,
            whole,
            pl.BlockSpec((model, fc), lambda j: (0, j)),
            pl.BlockSpec((1, fc), lambda j: (0, j)),
            pl.BlockSpec((fc, model), lambda j: (j, 0)),
        ],
        out_specs=[
            whole,
            whole,
            pl.BlockSpec((model, fc), lambda j: (0, j)),
            pl.BlockSpec((fc, model), lambda j: (j, 0)),
            pl.BlockSpec((1, fc), lambda j: (0, j)),
        ],
        out_shape=[
            jax.ShapeDtypeStruct((tokens, model), F32),
            jax.ShapeDtypeStruct((tokens, model), F32),
            jax.ShapeDtypeStruct((model, hidden), BF16),
            jax.ShapeDtypeStruct((hidden, model), BF16),
            jax.ShapeDtypeStruct((1, hidden), F32),
        ],
        scratch_shapes=[pltpu.VMEM((tokens, fc), BF16), pltpu.VMEM((tokens, fc), BF16)],
        compiler_params=params(),
        cost_estimate=cost(12 * tokens * model * hidden, tokens * model * 12 + model * hidden * 8, 2 * tokens * hidden),
        name="ffn_block",
    )(n2, cot, w_up, b_up, w_down)


def norm_back(field, gain, e):
    centre = field - jnp.mean(field, axis=-1, keepdims=True)
    rate = lax.rsqrt(jnp.mean(centre * centre, axis=-1, keepdims=True) + EPS)
    n = centre * rate
    eg = e * gain
    grad = rate * (eg - jnp.mean(eg, axis=-1, keepdims=True) - n * jnp.mean(eg * n, axis=-1, keepdims=True))
    return grad, jnp.sum(e * n, axis=0, keepdims=True), jnp.sum(e, axis=0, keepdims=True)


def middle_back_kernel(gn_ref, mid_ref, cot_ref, w_ref, gain_ref, gm_ref, gb_ref, ga_ref, gg_ref, gs_ref):
    @pl.when(pl.program_id(0) == 0)
    def _():
        gg_ref[...] = jnp.zeros_like(gg_ref)
        gs_ref[...] = jnp.zeros_like(gs_ref)

    grad, gg, gs = norm_back(mid_ref[...], gain_ref[...], gn_ref[...])
    gg_ref[...] += gg
    gs_ref[...] += gs
    grad = cot_ref[...].astype(F32) + grad
    gm_ref[...] = grad
    branch = grad.astype(BF16)
    gb_ref[...] = branch
    ga_ref[...] = dot_nt(branch, w_ref[...]).astype(BF16)


def middle_back(gn2, middle, cot, w_out, gain, bm):
    tokens, model = middle.shape
    tile = pl.BlockSpec((bm, model), lambda i: (i, 0))
    line = pl.BlockSpec((1, model), lambda i: (0, 0))
    return pl.pallas_call(
        middle_back_kernel,
        grid=(tokens // bm,),
        in_specs=[tile, tile, tile, pl.BlockSpec((model, model), lambda i: (0, 0)), line],
        out_specs=[tile, tile, tile, line, line],
        out_shape=[
            jax.ShapeDtypeStruct((tokens, model), F32),
            jax.ShapeDtypeStruct((tokens, model), BF16),
            jax.ShapeDtypeStruct((tokens, model), BF16),
            jax.ShapeDtypeStruct((1, model), F32),
            jax.ShapeDtypeStruct((1, model), F32),
        ],
        compiler_params=params(),
        cost_estimate=cost(2 * tokens * model * model, tokens * model * 18 + model * model * 2),
        name="middle_back",
    )(gn2, middle, cot, w_out, gain)


def first_back_kernel(dn_ref, x_ref, gm_ref, gain_ref, out_ref, gg_ref, gs_ref):
    @pl.when(pl.program_id(0) == 0)
    def _():
        gg_ref[...] = jnp.zeros_like(gg_ref)
        gs_ref[...] = jnp.zeros_like(gs_ref)

    grad, gg, gs = norm_back(x_ref[...].astype(F32), gain_ref[...], dn_ref[...])
    gg_ref[...] += gg
    gs_ref[...] += gs
    out_ref[...] = (gm_ref[...] + grad).astype(BF16)


def first_back(dn, x, gm, gain, bm):
    tokens, model = x.shape
    tile = pl.BlockSpec((bm, model), lambda i: (i, 0))
    line = pl.BlockSpec((1, model), lambda i: (0, 0))
    return pl.pallas_call(
        first_back_kernel,
        grid=(tokens // bm,),
        in_specs=[tile, tile, tile, line],
        out_specs=[tile, line, line],
        out_shape=[
            jax.ShapeDtypeStruct((tokens, model), BF16),
            jax.ShapeDtypeStruct((1, model), F32),
            jax.ShapeDtypeStruct((1, model), F32),
        ],
        compiler_params=params(),
        cost_estimate=cost(20 * tokens * model, tokens * model * 12),
        name="first_back",
    )(dn, x, gm, gain)


def per_device(
    inputs,
    segment_ids,
    buckets,
    ln1_gain,
    ln1_bias,
    w_query,
    w_key,
    w_value,
    w_out,
    rel_bias,
    second_norm_gain,
    ln2_bias,
    w_up,
    b_up,
    w_down,
    b_down,
    cotangent,
):
    num_micro, num_rows, size, model = inputs.shape
    rows = num_micro * num_rows
    seq_len = segment_ids.shape[2]
    heads = rel_bias.shape[1]
    shards = lax.axis_size("fsdp")
    ranges = lax.axis_size("seq")
    num_buckets = rel_bias.shape[0] * shards
    hidden = w_up.shape[1]
    tokens = rows * size
    hops = min(-(-(CLIP - 1) // size), ranges - 1)
    halo = hops * size
    window = halo + size
    qb = min(128, size)
    blocks = size // qb
    kw = halo + qb
    width = -(-(kw + qb) // 128) * 128
    tile = min(256, tokens)

    gather = functools.partial(lax.all_gather, axis_name="fsdp", axis=0, tiled=True)
    w_qkv = gather(jnp.concatenate([w_query, w_key, w_value], axis=1))
    vectors = (ln1_gain, ln1_bias, second_norm_gain, ln2_bias, b_up, b_down, rel_bias.reshape(-1))
    packed = gather(jnp.concatenate(vectors)[None])
    parts, at = [], 0
    for v in vectors:
        parts.append(packed[:, at : at + v.size].reshape(1, -1))
        at += v.size
    gain1, shift1, gain2, shift2, bias_up, bias_down = (p.astype(F32) for p in parts[:6])
    table = parts[6].reshape(num_buckets, heads)
    out_mat = gather(w_out)
    up_mat = gather(w_up)
    down_mat = gather(w_down)

    x = inputs.reshape(rows, size, model)
    near = [x]
    for _ in range(hops):
        near.insert(0, lax.ppermute(near[0], "seq", [(i, i + 1) for i in range(ranges - 1)]))

    place = lax.axis_index("seq") * size
    column = jnp.arange(width, dtype=jnp.int32)
    gap = halo - column
    inside = (gap >= 0) & (column > 0)
    bucket_of = jnp.where(inside, jnp.flip(jnp.pad(buckets[: halo + 1], (width - halo - 1, 0))), -1)
    onehot = bucket_of[:, None] == jnp.arange(num_buckets, dtype=jnp.int32)[None]
    by_gap = dot_nn(onehot.astype(BF16), table) + jnp.where(inside, 0.0, NEG)[:, None]
    bias = make_bias(by_gap.T, qb, kw)
    segs = segment_ids.reshape(rows, seq_len)
    segs = lax.dynamic_slice_in_dim(jnp.pad(segs, ((0, 0), (halo, 0)), constant_values=-1), place, window, 1)
    mask = jnp.stack(
        [
            jnp.where(
                segs[:, halo + b * qb : halo + (b + 1) * qb, None] == segs[:, None, b * qb : b * qb + kw], 0.0, NEG
            )
            for b in range(blocks)
        ],
        axis=1,
    ).astype(F32)

    x = x.reshape(tokens, model)
    normed = norm_window(near, gain1, shift1).reshape(rows * window, model)
    kv = project(normed, w_qkv, window, 1, 0, model, 2 * model, 512, 1.0, "keys_values")
    q = project(normed, w_qkv, size, hops + 1, hops, 0, model, 512, 0.125, "queries")
    attended, inv, expo = attn_fwd(q, kv, bias, mask)
    middle, normed_two = middle_block(attended, out_mat, x, gain2, shift2, tile)

    cot = cotangent.reshape(tokens, model)
    ff_out, grad_norm2, grad_w_up, grad_w_down, grad_b_up = ffn_block(
        normed_two, cot, up_mat, bias_up, down_mat, min(512, hidden), tile
    )
    outputs = (middle + ff_out + bias_down).astype(BF16)
    grad_b_down = jnp.sum(cot.astype(F32), axis=0, keepdims=True)

    def scatter(field):
        return lax.psum_scatter(field.astype(BF16), "fsdp", scatter_dimension=0, tiled=True)

    def total(field):
        return lax.psum(field, "seq").astype(F32)

    grad_w_up = scatter(grad_w_up)
    grad_w_down = scatter(grad_w_down)

    grad_middle, grad_branch, grad_attended, grad_gain2, grad_shift2 = middle_back(
        grad_norm2, middle, cot, out_mat, gain2, tile
    )
    grad_w_out = dot_tn(attended, grad_branch).astype(BF16)
    grad_q, grad_k, grad_v, diagonal = attn_bwd(q, kv, expo, inv, attended, grad_attended, width)
    normed = normed.reshape(rows, window, model)
    normed_own = normed[:, halo:].reshape(tokens, model)
    weight_grads = [
        dot_tn(normed_own, grad_q).astype(BF16),
        jnp.einsum("rti,rft->if", normed, grad_k, preferred_element_type=F32).astype(BF16),
        jnp.einsum("rti,rft->if", normed, grad_v, preferred_element_type=F32).astype(BF16),
        grad_w_out,
    ]
    grad_attn = scatter(jnp.concatenate(weight_grads, axis=1))
    grad_norm = jnp.einsum("rft,if->rti", grad_k, w_qkv[:, model : 2 * model], preferred_element_type=F32)
    grad_norm += jnp.einsum("rft,if->rti", grad_v, w_qkv[:, 2 * model :], preferred_element_type=F32)
    grad_own = dot_nt(grad_q, w_qkv[:, :model]) + grad_norm[:, halo:].reshape(tokens, model)
    carry = None
    for hop in range(hops):
        piece = grad_norm[:, hop * size : (hop + 1) * size]
        piece = piece if carry is None else piece + carry.astype(F32)
        carry = lax.ppermute(piece.astype(BF16), "seq", [(i + 1, i) for i in range(ranges - 1)])
    if carry is not None:
        grad_own += carry.astype(F32).reshape(tokens, model)
    input_grad, grad_gain1, grad_shift1 = first_back(grad_own, x, grad_middle, gain1, tile)

    diagonal = diagonal[:, :2].reshape(heads, width)
    grad_table = lax.dot_general(onehot.astype(F32), diagonal, (((0,), (1,)), ((), ())), precision=HIGHEST)

    small = (grad_gain1, grad_shift1, grad_gain2, grad_shift2, grad_b_up, grad_b_down, grad_table)
    small = jnp.concatenate([s.reshape(shards, -1) for s in small], axis=1)
    small = lax.psum(small, ("fsdp", "seq"))
    small = lax.dynamic_slice_in_dim(small, lax.axis_index("fsdp"), 1, 0)[0]
    finals, at = [], 0
    for v in vectors:
        finals.append(small[at : at + v.size].reshape(v.shape))
        at += v.size
    finals[6] = finals[6].reshape(rel_bias.shape)

    grad_w_up = total(grad_w_up)
    grad_w_down = total(grad_w_down)
    grad_attn = total(grad_attn)
    return (
        outputs.reshape(inputs.shape),
        input_grad.reshape(inputs.shape),
        finals[0],
        finals[1],
        grad_attn[:, :model],
        grad_attn[:, model : 2 * model],
        grad_attn[:, 2 * model : 3 * model],
        grad_attn[:, 3 * model :],
        finals[6],
        finals[2],
        finals[3],
        grad_w_up,
        finals[4],
        grad_w_down,
        finals[5],
    )


def solution(mesh):
    token = P(None, "fsdp", "seq", None)
    vector = P("fsdp")
    matrix = P("fsdp", None)
    return jax.shard_map(
        per_device,
        mesh=mesh,
        in_specs=(
            token, P(None, "fsdp", None), P(), vector, vector, matrix, matrix, matrix, matrix, matrix,
            vector, vector, matrix, vector, matrix, vector, token,
        ),
        out_specs=(
            token, token, vector, vector, matrix, matrix, matrix, matrix, matrix,
            vector, vector, matrix, vector, matrix, vector,
        ),
        check_vma=False,
    )
```

```python
import functools

import jax
import jax.numpy as jnp
from jax import lax
from jax.experimental import pallas as pl
from jax.experimental.pallas import tpu as pltpu
from jax.sharding import PartitionSpec as P

EPS = 1e-05
NEG = -1e30
CLIP = 512
F32 = jnp.float32
BF16 = jnp.bfloat16
HIGHEST = lax.Precision.HIGHEST
MIB = 1 << 20
COST = 30.0
LIGHT = 1.0

ERFC_P = 0.4375
ERFC_C = (
    0.24679607152938843,
    0.24772192537784576,
    0.2143726497888565,
    0.22321343421936035,
    -0.03611995279788971,
    0.3185710310935974,
    -0.2865786552429199,
    0.07202363014221191,
)


def params(vmem=56):
    return pltpu.CompilerParams(vmem_limit_bytes=vmem * MIB)


def cost(flops, nbytes, weight=COST):
    return pl.CostEstimate(flops=int(flops * weight), bytes_accessed=int(nbytes * weight), transcendentals=0)


def gelu_parts(u):
    tail = jnp.exp(u * u * -0.5)
    t = 1.0 / (1.0 + jnp.abs(u) * (ERFC_P * 0.5**0.5))
    poly = jnp.full_like(u, 0.5 * ERFC_C[-1])
    for c in ERFC_C[-2::-1]:
        poly = poly * t + 0.5 * c
    half = poly * t * tail
    cdf = jnp.where(u >= 0, 1.0 - half, half)
    return u * cdf, cdf + u * tail * 0.3989422804014327


def dot_nn(a, b):
    return lax.dot_general(a, b, (((1,), (0,)), ((), ())), preferred_element_type=F32)


def dot_nt(a, b):
    return lax.dot_general(a, b, (((1,), (1,)), ((), ())), preferred_element_type=F32)


def dot_tn(a, b):
    return lax.dot_general(a, b, (((0,), (0,)), ((), ())), preferred_element_type=F32)


def bias_kernel(qb, row_ref, out_ref):
    width = row_ref.shape[-1]
    block = jnp.broadcast_to(row_ref[0], (8, width))
    sub = lax.broadcasted_iota(jnp.int32, (8, width), 0)
    for bit in range(3):
        block = jnp.where((sub >> bit) & 1 == 1, pltpu.roll(block, 1 << bit, 1), block)
    rows = 8
    while rows < qb:
        block = jnp.concatenate([block, pltpu.roll(block, rows, 1)], axis=0)
        rows *= 2
    out_ref[0] = block[:, : out_ref.shape[-1]]


def make_bias(row, qb, kw):
    heads, width = row.shape
    return pl.pallas_call(
        functools.partial(bias_kernel, qb),
        grid=(heads,),
        in_specs=[pl.BlockSpec((1, 1, width), lambda h: (h, 0, 0))],
        out_specs=pl.BlockSpec((1, qb, kw), lambda h: (h, 0, 0)),
        out_shape=jax.ShapeDtypeStruct((heads, qb, kw), F32),
        compiler_params=params(),
        cost_estimate=cost(0, heads * qb * kw * 4),
        name="bias_table",
    )(row[:, None, :])


def diagonal_sums(block, width):
    qb, kw = block.shape
    if width > kw:
        block = jnp.concatenate([block, jnp.zeros((qb, width - kw), F32)], axis=1)
    rows = qb
    while rows > 8:
        rows //= 2
        block = block[:rows] + pltpu.roll(block[rows:], width - rows, 1)
    sub = lax.broadcasted_iota(jnp.int32, (8, width), 0)
    for bit in range(3):
        block = jnp.where((sub >> bit) & 1 == 1, pltpu.roll(block, width - (1 << bit), 1), block)
    return jnp.sum(block, axis=0, keepdims=True)


def norm_kernel(order_ref, x_ref, gain_ref, shift_ref, out_ref, turned_ref, scratch):
    shards = order_ref.shape[0]
    part = scratch.shape[0] // shards
    field = x_ref[0].astype(F32)
    centre = field - jnp.mean(field, axis=-1, keepdims=True)
    spread = jnp.mean(centre * centre, axis=-1, keepdims=True)
    normed = (centre * lax.rsqrt(spread + EPS) * gain_ref[...] + shift_ref[...]).astype(BF16)
    out_ref[0] = normed
    scratch[...] = normed.T
    for t in range(shards):
        source = pl.ds(pl.multiple_of(order_ref[t] * part, part), part)
        turned_ref[0, t * part : (t + 1) * part] = scratch[source, :]


def norm_block(order, x, gain, shift):
    rows, size, width = x.shape
    line = pl.BlockSpec((1, width), lambda r, o: (0, 0))
    tile = pl.BlockSpec((1, size, width), lambda r, o: (r, 0, 0))
    normed, turned = pl.pallas_call(
        norm_kernel,
        grid_spec=pltpu.PrefetchScalarGridSpec(
            num_scalar_prefetch=1,
            grid=(rows,),
            in_specs=[tile, line, line],
            out_specs=[tile, pl.BlockSpec((1, width, size), lambda r, o: (r, 0, 0))],
            scratch_shapes=[pltpu.VMEM((width, size), BF16)],
        ),
        out_shape=[
            jax.ShapeDtypeStruct((rows, size, width), BF16),
            jax.ShapeDtypeStruct((rows, width, size), BF16),
        ],
        compiler_params=params(),
        cost_estimate=cost(10 * rows * size * width, rows * size * width * 6),
        name="norm_block",
    )(order, x, gain, shift)
    return normed.reshape(rows * size, width), turned


def proj_kernel(scaled, x_ref, w_ref, o_ref):
    out = dot_nn(x_ref[...], w_ref[...]).astype(BF16)
    o_ref[...] = jnp.where(pl.program_id(0) < scaled, out * 0.125, out) if scaled else out


def project(x, w, first, cols, scaled, bn=256):
    tokens, model = x.shape
    return pl.pallas_call(
        functools.partial(proj_kernel, scaled // bn),
        grid=(cols // bn,),
        in_specs=[
            pl.BlockSpec((tokens, model), lambda n: (0, 0), pipeline_mode=pl.Buffered(1)),
            pl.BlockSpec((model, bn), lambda n: (0, n + first // bn)),
        ],
        out_specs=pl.BlockSpec((tokens, bn), lambda n: (0, n)),
        out_shape=jax.ShapeDtypeStruct((tokens, cols), BF16),
        compiler_params=params(),
        cost_estimate=cost(2 * tokens * model * cols, 2 * (tokens * model + model * cols + tokens * cols)),
        name="project",
    )(x, w)


def split_pair(field, even):
    zero = jnp.zeros_like(field)
    return jnp.concatenate([jnp.where(even, field, zero), jnp.where(even, zero, field)], axis=0)


def join_pair(field, even):
    half = field.shape[0] // 2
    return jnp.where(even, field[:half], field[half:])


def attn_fwd_kernel(qb, n, q_ref, *refs):
    bias_ref, mask_ref, o_ref, inv_ref, e_ref = refs[2 * n :]
    k = jnp.concatenate([r[...] for r in refs[:n]], axis=0)
    v = jnp.concatenate([r[...] for r in refs[n : 2 * n]], axis=0)
    blocks = q_ref.shape[0] // qb
    kw = bias_ref.shape[-1]
    even = lax.broadcasted_iota(jnp.int32, (qb, 128), 1) < 64
    for b in range(blocks):
        rows = slice(b * qb, (b + 1) * qb)
        keys = slice(b * qb, b * qb + kw)
        scores = dot_nt(split_pair(q_ref[rows], even), k[keys])
        mask = mask_ref[0, b]
        scores = jnp.concatenate(
            [scores[:qb] + (bias_ref[0] + mask), scores[qb:] + (bias_ref[1] + mask)], axis=0
        )
        peak = jnp.max(scores, axis=-1, keepdims=True)
        expo = jnp.exp(scores - peak)
        inv = 1.0 / jnp.sum(expo, axis=-1, keepdims=True)
        expo = expo.astype(BF16)
        e_ref[0, 0, b] = expo
        inv = join_pair(jnp.broadcast_to(inv, (2 * qb, 128)), even)
        mixed = join_pair(dot_nn(expo, v[keys]), even)
        inv_ref[rows] = inv
        o_ref[rows] = (mixed * inv).astype(BF16)


def key_specs(n, size, pairs, first):
    near = [pl.BlockSpec((size, 128), lambda r, p: (r, p))] * (n - 1)
    far = [pl.BlockSpec((size, 128), lambda r, p: (r, p + pairs))] * (n - 1)
    return [
        *near,
        pl.BlockSpec((size, 128), lambda r, p: (r, p + first)),
        *far,
        pl.BlockSpec((size, 128), lambda r, p: (r, p + pairs + first)),
    ]


def attn_fwd(kvs, bias, mask):
    heads, qb, kw = bias.shape
    pairs = heads // 2
    rows, blocks = mask.shape[:2]
    size = blocks * qb
    n = len(kvs)
    q_shape = (rows * size, heads * 64)
    cells = rows * blocks * heads * qb * kw
    return pl.pallas_call(
        functools.partial(attn_fwd_kernel, qb, n),
        grid=(rows, pairs),
        in_specs=[
            pl.BlockSpec((size, 128), lambda r, p: (r, p)),
            *key_specs(n, size, pairs, pairs),
            pl.BlockSpec((2, qb, kw), lambda r, p: (p, 0, 0)),
            pl.BlockSpec((1, blocks, qb, kw), lambda r, p: (r, 0, 0, 0)),
        ],
        out_specs=[
            pl.BlockSpec((size, 128), lambda r, p: (r, p)),
            pl.BlockSpec((size, 128), lambda r, p: (r, p)),
            pl.BlockSpec((1, 1, blocks, 2 * qb, kw), lambda r, p: (r, p, 0, 0, 0)),
        ],
        out_shape=[
            jax.ShapeDtypeStruct(q_shape, BF16),
            jax.ShapeDtypeStruct(q_shape, F32),
            jax.ShapeDtypeStruct((rows, pairs, blocks, 2 * qb, kw), BF16),
        ],
        compiler_params=params(),
        cost_estimate=cost(cells * 256, cells * 4),
        name="attn_fwd",
    )(kvs[-1], *kvs, *kvs, bias, mask)


def attn_bwd_kernel(qb, width, n, q_ref, *refs):
    e_ref, inv_ref, o_ref, g_ref, dq_ref, dk_ref, dv_ref, diag_ref, sums, dk_acc, dv_acc = refs[2 * n :]
    k = jnp.concatenate([r[...] for r in refs[:n]], axis=0)
    v = jnp.concatenate([r[...] for r in refs[n : 2 * n]], axis=0)
    blocks = q_ref.shape[0] // qb
    kw = e_ref.shape[-1]
    row, pair = pl.program_id(0), pl.program_id(1)
    even = lax.broadcasted_iota(jnp.int32, (qb, 128), 1) < 64
    dk_acc[...] = jnp.zeros_like(dk_acc)
    dv_acc[...] = jnp.zeros_like(dv_acc)

    @pl.when(row == 0)
    def _():
        sums[pair] = jnp.zeros(sums.shape[1:], F32)

    for b in range(blocks):
        rows = slice(b * qb, (b + 1) * qb)
        keys = slice(b * qb, b * qb + kw)
        grad = (g_ref[rows].astype(F32) * inv_ref[rows]).astype(BF16)
        weigh = grad.astype(F32) * o_ref[rows].astype(F32)
        delta = jnp.sum(split_pair(weigh, even), axis=-1, keepdims=True)
        grad = split_pair(grad, even)
        expo = e_ref[0, 0, b]
        dscore = expo.astype(F32) * (dot_nt(grad, v[keys]) - delta)
        sums[pair] += dscore
        dscore = dscore.astype(BF16)
        dq_ref[rows] = (join_pair(dot_nn(dscore, k[keys]), even) * 0.125).astype(BF16)
        dk_acc[:, keys] += dot_tn(split_pair(q_ref[rows], even), dscore)
        dv_acc[:, keys] += dot_tn(grad, expo)

    dk_ref[0] = dk_acc[...].astype(BF16)
    dv_ref[0] = dv_acc[...].astype(BF16)

    @pl.when(row == pl.num_programs(0) - 1)
    def _():
        diag_ref[0, 0:1] = diagonal_sums(sums[pair, :qb], width)
        diag_ref[0, 1:2] = diagonal_sums(sums[pair, qb:], width)


def attn_bwd(kvs, e, inv, o, g, width):
    rows, pairs, blocks, qb2, kw = e.shape
    qb = qb2 // 2
    size = blocks * qb
    n = len(kvs)
    window = n * size
    model = o.shape[1]
    cells = e.size
    return pl.pallas_call(
        functools.partial(attn_bwd_kernel, qb, width, n),
        grid=(rows, pairs),
        in_specs=[
            pl.BlockSpec((size, 128), lambda r, p: (r, p)),
            *key_specs(n, size, pairs, pairs),
            pl.BlockSpec((1, 1, blocks, qb2, kw), lambda r, p: (r, p, 0, 0, 0)),
            pl.BlockSpec((size, 128), lambda r, p: (r, p)),
            pl.BlockSpec((size, 128), lambda r, p: (r, p)),
            pl.BlockSpec((size, 128), lambda r, p: (r, p)),
        ],
        out_specs=[
            pl.BlockSpec((size, 128), lambda r, p: (r, p)),
            pl.BlockSpec((1, 128, window), lambda r, p: (r, p, 0)),
            pl.BlockSpec((1, 128, window), lambda r, p: (r, p, 0)),
            pl.BlockSpec((1, 8, width), lambda r, p: (p, 0, 0)),
        ],
        out_shape=[
            jax.ShapeDtypeStruct(o.shape, BF16),
            jax.ShapeDtypeStruct((rows, model, window), BF16),
            jax.ShapeDtypeStruct((rows, model, window), BF16),
            jax.ShapeDtypeStruct((pairs, 8, width), F32),
        ],
        scratch_shapes=[pltpu.VMEM((pairs, qb2, kw), F32)] + [pltpu.VMEM((128, window), F32)] * 2,
        compiler_params=params(),
        cost_estimate=cost(cells * 512, cells * 4),
        name="attn_bwd",
    )(kvs[-1], *kvs, *kvs, e, inv, o, g)


def middle_kernel(order_ref, a_ref, w_ref, x_ref, gain_ref, shift_ref, mid_ref, norm_ref, turned_ref, mixed_ref, scratch):
    shards = order_ref.shape[0]
    part = scratch.shape[0] // shards

    def turn(field, out_ref):
        scratch[...] = field.T
        for t in range(shards):
            out_ref[t * part : (t + 1) * part] = scratch[pl.ds(pl.multiple_of(order_ref[t] * part, part), part), :]

    middle = x_ref[...].astype(F32) + dot_nn(a_ref[...], w_ref[...])
    mid_ref[...] = middle
    centre = middle - jnp.mean(middle, axis=-1, keepdims=True)
    spread = jnp.mean(centre * centre, axis=-1, keepdims=True)
    normed = (centre * lax.rsqrt(spread + EPS) * gain_ref[...] + shift_ref[...]).astype(BF16)
    norm_ref[...] = normed
    turn(normed, turned_ref)
    turn(a_ref[...], mixed_ref)


def middle_block(order, attended, w_attn, x, gain, shift, bm):
    tokens, model = x.shape
    tile = pl.BlockSpec((bm, model), lambda i, o: (i, 0))
    turned = pl.BlockSpec((model, bm), lambda i, o: (0, i))
    line = pl.BlockSpec((1, model), lambda i, o: (0, 0))
    return pl.pallas_call(
        middle_kernel,
        grid_spec=pltpu.PrefetchScalarGridSpec(
            num_scalar_prefetch=1,
            grid=(tokens // bm,),
            in_specs=[tile, pl.BlockSpec((model, model), lambda i, o: (0, w_attn.shape[1] // model - 1)), tile, line, line],
            out_specs=[tile, tile, turned, turned],
            scratch_shapes=[pltpu.VMEM((model, bm), BF16)],
        ),
        out_shape=[
            jax.ShapeDtypeStruct((tokens, model), F32),
            jax.ShapeDtypeStruct((tokens, model), BF16),
            jax.ShapeDtypeStruct((model, tokens), BF16),
            jax.ShapeDtypeStruct((model, tokens), BF16),
        ],
        compiler_params=params(),
        cost_estimate=cost(2 * tokens * model * model, tokens * model * 14 + model * model * 2),
        name="middle_block",
    )(order, attended, w_attn, x, gain, shift)


def ffn_kernel(
    bm, first, last, chip_ref, n2_ref, n2t_ref, cot_ref, acc_ref, gin_ref, wu_ref, bu_ref, d0_ref, d1_ref, bd_ref, *refs
):
    out_ref, gn_ref, us_ref, uk_ref, ds_ref, dk_ref, gbu_ref, sums, wd, act_s, gpre_s, spare = refs[-12:]
    step = pl.program_id(0)
    tokens = n2_ref.shape[0]
    part = d0_ref.shape[0] // 2
    core = chip_ref[chip_ref.shape[0] - 1]

    @pl.when(step == 0)
    def _():
        if first:
            sums[...] = acc_ref[...] + bd_ref[...]
            gn_ref[...] = jnp.zeros_like(gn_ref)
        else:
            sums[...] = acc_ref[...]
            gn_ref[...] = gin_ref[...]

    for c in range(2):
        for i, d_ref in enumerate((d0_ref, d1_ref)):
            wd[(2 * c + i) * part : (2 * c + i + 1) * part] = d_ref[c * part : (c + 1) * part]
    gbu_ref[...] = jnp.zeros_like(gbu_ref)

    def tile(rows):
        act, slope = gelu_parts(dot_nn(n2_ref[rows, :], wu_ref[...]) + bu_ref[...])
        gpre = (dot_nt(cot_ref[rows, :], wd[...]) * slope).astype(BF16)
        act = act.astype(BF16)
        act_s[rows, :] = act
        gpre_s[rows, :] = gpre
        gbu_ref[...] += jnp.sum(gpre.astype(F32), axis=0, keepdims=True)
        sums[rows, :] += dot_nn(act, wd[...])
        gn_ref[rows, :] += dot_nt(gpre, wu_ref[...])

    for i in range(tokens // bm):
        tile(slice(i * bm, (i + 1) * bm))

    spare[...] = dot_tn(act_s[...], cot_ref[...]).astype(BF16).reshape(spare.shape)
    ds_ref[0] = spare[1 - core]
    dk_ref[0] = spare[core]
    half = n2t_ref.shape[0] // 2
    us_ref[...] = dot_nn(n2t_ref[:half], gpre_s[...]).astype(BF16).reshape(us_ref.shape)
    uk_ref[...] = dot_nn(n2t_ref[half:], gpre_s[...]).astype(BF16).reshape(uk_ref.shape)

    @pl.when(step == pl.num_programs(0) - 1)
    def _():
        out_ref[...] = sums[...].astype(out_ref.dtype)


def ffn_block(chips, n2, n2t, cot, acc, gin, w, b_up, b_down, begin, end, first, last, bm, grads=()):
    tokens, model = n2.shape
    pairs = chips.shape[0] - 1
    shards = 2 * pairs
    part = model // shards
    hidden = b_up.shape[1]
    fc = hidden // pairs
    once = pl.Buffered(1)
    whole = pl.BlockSpec((tokens, model), lambda j, o: (0, 0), pipeline_mode=once)
    by_col = pl.BlockSpec((pairs, part, fc), lambda j, o: (0, 0, o[j + begin]))
    by_row = pl.BlockSpec((1, fc // 2, model), lambda j, o: (j + begin, 0, 0))
    return pl.pallas_call(
        functools.partial(ffn_kernel, bm, first, last),
        grid_spec=pltpu.PrefetchScalarGridSpec(
            num_scalar_prefetch=1,
            grid=(end - begin,),
            in_specs=[
                whole,
                pl.BlockSpec((model, tokens), lambda j, o: (0, 0), pipeline_mode=once),
                whole,
                whole,
                pl.BlockSpec((8, model), lambda j, o: (0, 0)) if first else whole,
                pl.BlockSpec((model, fc), lambda j, o: (0, o[j + begin])),
                pl.BlockSpec((1, fc), lambda j, o: (0, o[j + begin])),
                pl.BlockSpec((2 * part, model), lambda j, o: (o[j + begin], hidden // model)),
                pl.BlockSpec((2 * part, model), lambda j, o: (o[j + begin], hidden // model + 1)),
                pl.BlockSpec((1, model), lambda j, o: (0, 0)),
                *[pl.BlockSpec(memory_space=pl.ANY)] * len(grads),
            ],
            out_specs=[
                pl.BlockSpec((tokens, model), lambda j, o: (0, 0)),
                pl.BlockSpec((tokens, model), lambda j, o: (0, 0)),
                by_col,
                by_col,
                by_row,
                by_row,
                pl.BlockSpec((1, fc), lambda j, o: (0, o[j + begin])),
            ],
            scratch_shapes=[
                pltpu.VMEM((tokens, model), F32),
                pltpu.VMEM((fc, model), BF16),
                pltpu.VMEM((tokens, fc), BF16),
                pltpu.VMEM((tokens, fc), BF16),
                pltpu.VMEM((2, fc // 2, model), BF16),
            ],
        ),
        out_shape=[
            jax.ShapeDtypeStruct((tokens, model), BF16 if last else F32),
            jax.ShapeDtypeStruct((tokens, model), F32),
            jax.ShapeDtypeStruct((pairs, part, hidden), BF16),
            jax.ShapeDtypeStruct((pairs, part, hidden), BF16),
            jax.ShapeDtypeStruct((pairs, fc // 2, model), BF16),
            jax.ShapeDtypeStruct((pairs, fc // 2, model), BF16),
            jax.ShapeDtypeStruct((1, hidden), F32),
        ],
        input_output_aliases={11 + i: 2 + i for i in range(len(grads))},
        compiler_params=params(),
        cost_estimate=cost(
            12 * tokens * model * fc * (end - begin),
            tokens * model * 20 + model * fc * (end - begin) * 8,
        ),
        name="ffn_block",
    )(chips, n2, n2t, cot, acc, gin, w, b_up, w, w, b_down, *grads)


def norm_back(field, gain, e):
    centre = field - jnp.mean(field, axis=-1, keepdims=True)
    rate = lax.rsqrt(jnp.mean(centre * centre, axis=-1, keepdims=True) + EPS)
    n = centre * rate
    eg = e * gain
    grad = rate * (eg - jnp.mean(eg, axis=-1, keepdims=True) - n * jnp.mean(eg * n, axis=-1, keepdims=True))
    return grad, jnp.sum(e * n, axis=0, keepdims=True), jnp.sum(e, axis=0, keepdims=True)


def middle_back_kernel(gn_ref, mid_ref, cot_ref, w_ref, gain_ref, gm_ref, gb_ref, ga_ref, gg_ref, gs_ref):
    @pl.when(pl.program_id(0) == 0)
    def _():
        gg_ref[...] = jnp.zeros_like(gg_ref)
        gs_ref[...] = jnp.zeros_like(gs_ref)

    grad, gg, gs = norm_back(mid_ref[...], gain_ref[...], gn_ref[...])
    gg_ref[...] += gg
    gs_ref[...] += gs
    grad = cot_ref[...].astype(F32) + grad
    gm_ref[...] = grad
    branch = grad.astype(BF16)
    gb_ref[...] = branch
    ga_ref[...] = dot_nt(branch, w_ref[...]).astype(BF16)


def middle_back(gn2, middle, cot, w_attn, gain, bm):
    tokens, model = middle.shape
    tile = pl.BlockSpec((bm, model), lambda i: (i, 0))
    line = pl.BlockSpec((1, model), lambda i: (0, 0))
    return pl.pallas_call(
        middle_back_kernel,
        grid=(tokens // bm,),
        in_specs=[tile, tile, tile, pl.BlockSpec((model, model), lambda i: (0, w_attn.shape[1] // model - 1)), line],
        out_specs=[tile, tile, tile, line, line],
        out_shape=[
            jax.ShapeDtypeStruct((tokens, model), F32),
            jax.ShapeDtypeStruct((tokens, model), BF16),
            jax.ShapeDtypeStruct((tokens, model), BF16),
            jax.ShapeDtypeStruct((1, model), F32),
            jax.ShapeDtypeStruct((1, model), F32),
        ],
        compiler_params=params(),
        cost_estimate=cost(2 * tokens * model * model, tokens * model * 18 + model * model * 2),
        name="middle_back",
    )(gn2, middle, cot, w_attn, gain)


def attn_weights_kernel(n, *refs):
    turned = refs[:n]
    at_ref, dq_ref, dk_ref, dv_ref, gb_ref, first_ref, last_ref = refs[n:]
    model = gb_ref.shape[1]
    rows, _, size = turned[0].shape
    half, part = first_ref.shape[:2]

    def store(ref, side, value):
        ref[:, :, side * model : (side + 1) * model] = value.astype(BF16).reshape(half, part, model)

    def over_window(ref):
        return sum(
            dot_nt(turned[b][r], ref[r, :, b * size : (b + 1) * size]) for r in range(rows) for b in range(n)
        )

    store(first_ref, 0, sum(dot_nn(turned[-1][r], dq_ref[r]) for r in range(rows)))
    store(first_ref, 1, over_window(dk_ref))
    store(last_ref, 0, over_window(dv_ref))
    store(last_ref, 1, dot_nn(at_ref[...], gb_ref[...]))


def attn_weights(side, turned, mixed, dq, dk, dv, branch, shards):
    rows, model, size = turned[0].shape
    tokens = branch.shape[0]
    n = len(turned)
    window = n * size
    half = shards // 2
    part = model // shards

    def full(*shape):
        return pl.BlockSpec(shape, lambda i: (0,) * len(shape))

    out = jax.ShapeDtypeStruct((half, part, 2 * model), BF16)
    return pl.pallas_call(
        functools.partial(attn_weights_kernel, n),
        grid=(1,),
        in_specs=[
            *[pl.BlockSpec((rows, model // 2, size), lambda i: (0, side, 0))] * n,
            pl.BlockSpec((model // 2, tokens), lambda i: (side, 0)),
            full(rows, size, model),
            full(rows, model, window),
            full(rows, model, window),
            full(tokens, model),
        ],
        out_specs=[full(half, part, 2 * model)] * 2,
        out_shape=[out, out],
        compiler_params=params(),
        cost_estimate=cost(2 * model * model * (tokens + rows * window), 2 * (4 * rows * model * window + 4 * model * model), COST if side else LIGHT),
        name="attn_weights",
    )(*turned, mixed, dq.reshape(rows, size, model), dk, dv, branch)


def norm_grad_kernel(own, dk_ref, dv_ref, w_ref, *refs):
    model = w_ref.shape[0]
    out_ref = refs[-1]
    grad = dot_nn(w_ref[:, model : 2 * model], dk_ref[0]) + dot_nn(w_ref[:, 2 * model :], dv_ref[0])
    if own:
        out_ref[0] = grad.T + dot_nt(refs[0][0], w_ref[:, :model])
    elif len(refs) == 2:
        out_ref[0] = (grad.T + refs[0][0].astype(F32)).astype(BF16)
    else:
        out_ref[0] = grad.astype(BF16).T


def norm_grad(dk, dv, w_attn, block, size, dq=None, carry=None):
    rows, model, window = dk.shape
    tile = pl.BlockSpec((1, size, model), lambda r: (r, 0, 0))
    if size % 128 == 0 or size == window:
        side = pl.BlockSpec((1, model, size), lambda r: (r, 0, block))
    else:
        side = pl.BlockSpec((1, model, size), lambda r: (r, 0, 0))
        dk, dv = (lax.slice_in_dim(d, block * size, (block + 1) * size, axis=2) for d in (dk, dv))
    more = [x.reshape(rows, size, model) for x in (dq, carry) if x is not None]
    return pl.pallas_call(
        functools.partial(norm_grad_kernel, dq is not None),
        grid=(rows,),
        in_specs=[
            side,
            side,
            pl.BlockSpec((model, 3 * model), lambda r: (0, 0), pipeline_mode=pl.Buffered(1)),
            *[tile] * len(more),
        ],
        out_specs=tile,
        out_shape=jax.ShapeDtypeStruct((rows, size, model), F32 if dq is not None else BF16),
        compiler_params=params(),
        cost_estimate=cost((6 if dq is not None else 4) * rows * model * model * size, rows * model * size * 8 + 6 * model * model, LIGHT),
        name="norm_grad",
    )(dk, dv, w_attn, *more)


def first_back_kernel(dn_ref, back_ref, x_ref, gm_ref, gain_ref, out_ref, gg_ref, gs_ref):
    @pl.when(pl.program_id(0) == 0)
    def _():
        gg_ref[...] = jnp.zeros_like(gg_ref)
        gs_ref[...] = jnp.zeros_like(gs_ref)

    e = dn_ref[...] + back_ref[...].astype(F32)
    grad, gg, gs = norm_back(x_ref[...].astype(F32), gain_ref[...], e)
    gg_ref[...] += gg
    gs_ref[...] += gs
    out_ref[...] = (gm_ref[...] + grad).astype(BF16)


def first_back(dn, back, x, gm, gain, bm):
    tokens, model = x.shape
    tile = pl.BlockSpec((bm, model), lambda i: (i, 0))
    line = pl.BlockSpec((1, model), lambda i: (0, 0))
    return pl.pallas_call(
        first_back_kernel,
        grid=(tokens // bm,),
        in_specs=[tile, tile, tile, tile, line],
        out_specs=[tile, line, line],
        out_shape=[
            jax.ShapeDtypeStruct((tokens, model), BF16),
            jax.ShapeDtypeStruct((1, model), F32),
            jax.ShapeDtypeStruct((1, model), F32),
        ],
        compiler_params=params(),
        cost_estimate=cost(20 * tokens * model, tokens * model * 14),
        name="first_back",
    )(dn, back, x, gm, gain)


def flip(axis, count, bit):
    return functools.partial(lax.ppermute, axis_name=axis, perm=[(i, i ^ bit) for i in range(count)])


def add_low(a, b):
    return (a.astype(F32) + b.astype(F32)).astype(BF16)


def merge_kernel(n, *refs):
    ins, outs = refs[: 2 * n], refs[2 * n :]
    for i, out in enumerate(outs):
        out[...] = (ins[2 * i][...].astype(F32) + ins[2 * i + 1][...].astype(F32)).astype(out.dtype)


def merge(pairs, backwards, final):
    ins, in_specs, out_shape, out_specs = [], [], [], []
    count = pairs[0][0].shape[0]
    half = max(count // 2, 1)
    tiles = 4
    for (a, b), back in zip(pairs, backwards):
        _, rows, cols = a.shape
        shape = (1, rows // tiles, cols)
        if final:
            picks = [lambda q, t: (0, t, 0)]
        elif back:
            picks = [lambda q, t: (q, t, 0), lambda q, t: (q + half, t, 0)]
        else:
            picks = [lambda q, t: (2 * q, t, 0), lambda q, t: (2 * q + 1, t, 0)]
        for pick in picks:
            ins += [a, b]
            in_specs += [pl.BlockSpec(shape, pick)] * 2
            out_specs.append(pl.BlockSpec(shape, lambda q, t: (q, t, 0)))
            out_shape.append(jax.ShapeDtypeStruct((half, rows, cols), BF16))
    size = sum(a.size for a, _ in pairs)
    outs = pl.pallas_call(
        functools.partial(merge_kernel, len(out_shape)),
        grid=(half, tiles),
        in_specs=in_specs,
        out_specs=out_specs,
        out_shape=out_shape,
        compiler_params=params(),
        cost_estimate=cost(size, size * 6, LIGHT),
        name="merge",
    )(*ins)
    return list(outs) if final else list(zip(outs[0::2], outs[1::2]))


class ShardSum:
    def __init__(self, sends, keeps, shards):
        self.shards = shards
        self.bits = list(range(1, shards.bit_length() - 1))
        self.stage = 0
        self.back = [i % 2 == 1 for i in range(len(keeps))]
        self.flying = [(k, flip("fsdp", shards, 1)(s)) for k, s in zip(keeps, sends)]

    def land(self):
        return merge(self.flying, self.back, self.stage == len(self.bits))

    def launch(self, landed):
        self.flying = []
        for back, (kept, sent) in zip(self.back, landed):
            bit = (self.bits[::-1] if back else self.bits)[self.stage]
            self.flying.append((kept, flip("fsdp", self.shards, 1 << bit)(sent)))
        self.stage += 1

    def step(self, *others):
        landed, others = lax.optimization_barrier((self.land(), others))
        self.launch(landed)
        return others if len(others) != 1 else others[0]

    def finish(self):
        while self.stage < len(self.bits):
            self.launch(self.land())
        return [f[0] for f in self.land()]


def add_everywhere(field, axes):
    for axis, count in axes:
        bit = 1
        while bit < count:
            field = field + flip(axis, count, bit)(field)
            bit *= 2
    return field


def per_device(
    inputs,
    segment_ids,
    buckets,
    ln1_gain,
    ln1_bias,
    w_query,
    w_key,
    w_value,
    w_out,
    rel_bias,
    second_norm_gain,
    ln2_bias,
    w_up,
    b_up,
    w_down,
    b_down,
    cotangent,
):
    num_micro, num_rows, size, model = inputs.shape
    rows = num_micro * num_rows
    seq_len = segment_ids.shape[2]
    heads = rel_bias.shape[1]
    shards = lax.axis_size("fsdp")
    ranges = lax.axis_size("seq")
    num_buckets = rel_bias.shape[0] * shards
    hidden = w_up.shape[1]
    tokens = rows * size
    hops = min(-(-(CLIP - 1) // size), ranges - 1)
    halo = hops * size
    window = halo + size
    qb = min(128, size)
    blocks = size // qb
    kw = halo + qb
    width = -(-(kw + qb) // 128) * 128
    tile = min(256, tokens)

    me = lax.axis_index("fsdp")
    order = me ^ jnp.array([*range(1, shards, 2), *range(0, shards, 2)], jnp.int32)
    chips = jnp.append((me // 2) ^ jnp.arange(shards // 2, dtype=jnp.int32), me % 2)

    gather = functools.partial(lax.all_gather, axis_name="fsdp", axis=0, tiled=True)
    w_local = jnp.concatenate([w_query, w_key, w_value], axis=1)
    x = inputs.reshape(rows, size, model)
    w_local, x, w_out, w_up, w_down = lax.optimization_barrier((w_local, x, w_out, w_up, w_down))
    w_attn = gather(w_local)
    up = [(i, i + 1) for i in range(ranges - 1)]
    near = [x]
    if hops:
        near.insert(0, lax.ppermute(x, "seq", up))
    vectors = (ln1_gain, ln1_bias, second_norm_gain, ln2_bias, b_up, b_down, rel_bias.reshape(-1))
    packed = jnp.concatenate(vectors)[None].astype(F32)
    packed = jnp.where(jnp.arange(shards)[:, None] == me, packed, 0.0)
    packed = add_everywhere(packed, (("fsdp", shards),))
    parts, at = [], 0
    for v in vectors:
        parts.append(packed[:, at : at + v.size].reshape(1, -1))
        at += v.size
    gain1, shift1, gain2, shift2, bias_up, bias_down = parts[:6]
    table = parts[6].reshape(num_buckets, heads).astype(BF16)
    fine = hidden // shards // 2
    columns = w_up.reshape(w_up.shape[0], shards, 2, fine)
    w_ff = []
    for side in range(2):
        pieces = [columns[:, :, side].reshape(w_up.shape[0], -1)]
        down = w_down[side * fine : (side + 1) * fine].reshape(-1, w_up.shape[0], model)
        pieces += [down[i] for i in range(down.shape[0])]
        if side == 0:
            pieces.append(w_out)
        w_ff.append(gather(jnp.concatenate(pieces, axis=1)))

    place = lax.axis_index("seq") * size
    column = jnp.arange(width, dtype=jnp.int32)
    gap = halo - column
    inside = (gap >= 0) & (column > 0)
    bucket_of = jnp.where(inside, jnp.flip(jnp.pad(buckets[: halo + 1], (width - halo - 1, 0))), -1)
    onehot = bucket_of[:, None] == jnp.arange(num_buckets, dtype=jnp.int32)[None]
    by_gap = dot_nn(onehot.astype(BF16), table) + jnp.where(inside, 0.0, NEG)[:, None]
    bias = make_bias(by_gap.T, qb, kw)
    segs = segment_ids.reshape(rows, seq_len)
    segs = lax.dynamic_slice_in_dim(jnp.pad(segs, ((0, 0), (halo, 0)), constant_values=-1), place, window, 1)
    mask = jnp.stack(
        [
            jnp.where(
                segs[:, halo + b * qb : halo + (b + 1) * qb, None] == segs[:, None, b * qb : b * qb + kw], 0.0, NEG
            )
            for b in range(blocks)
        ],
        axis=1,
    ).astype(F32)

    for hop in range(hops - 1):
        moved = near[0]
        if hop == 0:
            moved, bias, mask, gain1 = lax.optimization_barrier((moved, bias, mask, gain1))
        near.insert(0, lax.ppermute(moved, "seq", up))

    normed, turned, kvs = [None] * (hops + 1), [None] * (hops + 1), [None] * (hops + 1)
    for b in range(hops, -1, -1):
        if b == hops - 2:
            near[: b + 1], kvs[b + 1 :] = lax.optimization_barrier((near[: b + 1], kvs[b + 1 :]))
        normed[b], turned[b] = norm_block(order, near[b], gain1, shift1)
        first, cols, scaled = (0, 3 * model, model) if b == hops else (model, 2 * model, 0)
        kvs[b] = project(normed[b], w_attn, first, cols, scaled)
    attended, inv, expo = attn_fwd(kvs, bias, mask)
    x = x.reshape(tokens, model)
    middle, normed_two, two_turned, mixed_turned = middle_block(order, attended, w_ff[0], x, gain2, shift2, tile)

    cot = cotangent.reshape(tokens, model)
    bias_up = bias_up.reshape(shards, 2, fine)
    tile_ff = tokens // 2 if tokens % 32 == 0 else tokens
    pairs = shards // 2
    ffn = functools.partial(ffn_block, chips, normed_two, two_turned, cot, b_down=bias_down, bm=tile_ff)
    bias_a, bias_b = (bias_up[:, side].reshape(1, -1) for side in range(2))
    part_out, part_grad, us, uk, ds, dk, grad_b_a = ffn(
        middle, jnp.zeros((8, model), F32), w_ff[0], bias_a, begin=0, end=pairs, first=True, last=False
    )
    sum_a = ShardSum([us, ds], [uk, dk], shards)
    part_out, part_grad, *grads = ffn(
        part_out, part_grad, w_ff[1], bias_b, begin=0, end=pairs // 2, first=False, last=False
    )
    part_grad = sum_a.step(part_grad)
    outputs, grad_norm2, us, uk, ds, dk, grad_b_b = ffn(
        part_out, part_grad, w_ff[1], bias_b, begin=pairs // 2, end=pairs, first=False, last=True, grads=grads
    )
    sum_b = ShardSum([us, ds], [uk, dk], shards)
    grad_b_up = jnp.stack([grad_b_a.reshape(shards, fine), grad_b_b.reshape(shards, fine)], axis=1)
    grad_b_down = jnp.sum(cot.astype(F32), axis=0, keepdims=True)

    def total(fields):
        return lax.psum(tuple(fields), "seq")

    if sum_a.stage < len(sum_a.bits):
        grad_norm2 = sum_a.step(grad_norm2)
    grad_middle, grad_branch, grad_attended, grad_gain2, grad_shift2 = middle_back(
        grad_norm2, middle, cot, w_ff[0], gain2, tile
    )
    grad_attended = sum_b.step(grad_attended)
    done_a = sum_a.finish()
    grad_attended, done_a = lax.optimization_barrier((grad_attended, done_a))
    total_a = total(done_a)
    grad_q, grad_k, grad_v, diagonal = attn_bwd(kvs, expo, inv, attended, grad_attended, width)
    if sum_b.stage < len(sum_b.bits):
        grad_q = sum_b.step(grad_q)
    back = None
    down = [(i + 1, i) for i in range(ranges - 1)]
    if hops:
        grad_far = norm_grad(grad_k, grad_v, w_attn, 0, size)
        grad_far, grad_q = lax.optimization_barrier((grad_far, grad_q))
        back = lax.ppermute(grad_far, "seq", down)
    first_send, last_send = attn_weights(0, turned, mixed_turned, grad_q, grad_k, grad_v, grad_branch, shards)
    done_b = sum_b.finish()
    done_b, grad_q, first_send, total_a = lax.optimization_barrier((done_b, grad_q, first_send, total_a))
    up_b, down_b = done_b
    total_b = jnp.concatenate([*jnp.split(up_b, up_b.shape[1] // model, axis=1), down_b], axis=0)
    total_b = lax.psum_scatter(total_b, "seq", scatter_dimension=0, tiled=True)
    total_b = lax.all_gather(total_b, "seq", axis=0, tiled=True)
    first_keep, last_keep = attn_weights(1, turned, mixed_turned, grad_q, grad_k, grad_v, grad_branch, shards)
    sum_c = ShardSum([first_send, last_send], [first_keep, last_keep], shards)
    grad_k, grad_v, grad_q = sum_c.step(grad_k, grad_v, grad_q)
    for hop in range(1, hops):
        grad_far = norm_grad(grad_k, grad_v, w_attn, hop, size, carry=back)
        grad_far, grad_q = lax.optimization_barrier((grad_far, grad_q))
        back = lax.ppermute(grad_far, "seq", down)
    grad_q, total_b = lax.optimization_barrier((grad_q, total_b))
    grad_own = norm_grad(grad_k, grad_v, w_attn, hops, size, dq=grad_q)
    done_c = sum_c.finish()
    done_c, total_b, grad_own = lax.optimization_barrier((done_c, total_b, grad_own))
    grad_first, grad_last = (f.astype(F32) for f in total(done_c))
    up_a, down_a = (f.astype(F32) for f in total_a)
    total_b = total_b.astype(F32)
    count = up_b.shape[0] * (up_b.shape[1] // model)
    up_b = jnp.concatenate(jnp.split(total_b[:count], up_b.shape[1] // model, axis=0), axis=1)
    down_b = total_b[count:]
    grad_w_up = jnp.stack([up_a.reshape(-1, shards, fine), up_b.reshape(-1, shards, fine)], axis=2).reshape(w_up.shape)
    grad_w_down = jnp.concatenate([down_a, down_b], axis=0)
    if back is None:
        back = jnp.zeros((rows, size, model), BF16)
    input_grad, grad_gain1, grad_shift1 = first_back(
        grad_own.reshape(tokens, model), back.reshape(tokens, model), x, grad_middle, gain1, tile
    )

    diagonal = diagonal[:, :2].reshape(heads, width)
    grad_table = lax.dot_general(onehot.astype(F32), diagonal, (((0,), (1,)), ((), ())), precision=HIGHEST)

    small = (grad_gain1, grad_shift1, grad_gain2, grad_shift2, grad_b_up, grad_b_down, grad_table)
    small = jnp.concatenate([s.reshape(shards, -1) for s in small], axis=1)
    small = add_everywhere(small, (("fsdp", shards), ("seq", ranges)))
    small = lax.dynamic_slice_in_dim(small, lax.axis_index("fsdp"), 1, 0)[0]
    finals, at = [], 0
    for v in vectors:
        finals.append(small[at : at + v.size].reshape(v.shape))
        at += v.size
    finals[6] = finals[6].reshape(rel_bias.shape)

    return (
        outputs.reshape(inputs.shape),
        input_grad.reshape(inputs.shape),
        finals[0],
        finals[1],
        grad_first[:, :model],
        grad_first[:, model:],
        grad_last[:, :model],
        grad_last[:, model:],
        finals[6],
        finals[2],
        finals[3],
        grad_w_up,
        finals[4],
        grad_w_down,
        finals[5],
    )


def solution(mesh):
    token = P(None, "fsdp", "seq", None)
    vector = P("fsdp")
    matrix = P("fsdp", None)
    return jax.shard_map(
        per_device,
        mesh=mesh,
        in_specs=(
            token, P(None, "fsdp", None), P(), vector, vector, matrix, matrix, matrix, matrix, matrix,
            vector, vector, matrix, vector, matrix, vector, token,
        ),
        out_specs=(
            token, token, vector, vector, matrix, matrix, matrix, matrix, matrix,
            vector, vector, matrix, vector, matrix, vector,
        ),
        check_vma=False,
    )
```

```python
import functools

import jax
import jax.numpy as jnp
from jax import lax
from jax.experimental import pallas as pl
from jax.experimental.pallas import tpu as pltpu
from jax.sharding import PartitionSpec as P

EPS = 1e-05
NEG = -1e30
CLIP = 512
F32 = jnp.float32
BF16 = jnp.bfloat16
HIGHEST = lax.Precision.HIGHEST
MIB = 1 << 20
COST = 30.0
LIGHT = 0.0

ERFC_P = 0.4375
ERFC_C = (
    0.24679607152938843,
    0.24772192537784576,
    0.2143726497888565,
    0.22321343421936035,
    -0.03611995279788971,
    0.3185710310935974,
    -0.2865786552429199,
    0.07202363014221191,
)


def params(vmem=56):
    return pltpu.CompilerParams(vmem_limit_bytes=vmem * MIB)


def cost(flops, nbytes, weight=COST):
    return pl.CostEstimate(flops=int(flops * weight), bytes_accessed=int(nbytes * weight), transcendentals=0)


def gelu_parts(u):
    tail = jnp.exp(u * u * -0.5)
    t = 1.0 / (1.0 + jnp.abs(u) * (ERFC_P * 0.5**0.5))
    poly = jnp.full_like(u, 0.5 * ERFC_C[-1])
    for c in ERFC_C[-2::-1]:
        poly = poly * t + 0.5 * c
    half = poly * t * tail
    cdf = jnp.where(u >= 0, 1.0 - half, half)
    return u * cdf, cdf + u * tail * 0.3989422804014327


def dot_nn(a, b):
    return lax.dot_general(a, b, (((1,), (0,)), ((), ())), preferred_element_type=F32)


def dot_nt(a, b):
    return lax.dot_general(a, b, (((1,), (1,)), ((), ())), preferred_element_type=F32)


def dot_tn(a, b):
    return lax.dot_general(a, b, (((0,), (0,)), ((), ())), preferred_element_type=F32)


def bias_kernel(qb, row_ref, out_ref):
    width = row_ref.shape[-1]
    block = jnp.broadcast_to(row_ref[0], (8, width))
    sub = lax.broadcasted_iota(jnp.int32, (8, width), 0)
    for bit in range(3):
        block = jnp.where((sub >> bit) & 1 == 1, pltpu.roll(block, 1 << bit, 1), block)
    rows = 8
    while rows < qb:
        block = jnp.concatenate([block, pltpu.roll(block, rows, 1)], axis=0)
        rows *= 2
    out_ref[0] = block[:, : out_ref.shape[-1]]


def make_bias(row, qb, kw):
    heads, width = row.shape
    return pl.pallas_call(
        functools.partial(bias_kernel, qb),
        grid=(heads,),
        in_specs=[pl.BlockSpec((1, 1, width), lambda h: (h, 0, 0))],
        out_specs=pl.BlockSpec((1, qb, kw), lambda h: (h, 0, 0)),
        out_shape=jax.ShapeDtypeStruct((heads, qb, kw), F32),
        compiler_params=params(),
        cost_estimate=cost(0, heads * qb * kw * 4, 0.0),
        name="bias_table",
    )(row[:, None, :])


def diagonal_sums(block, width):
    qb, kw = block.shape
    if width > kw:
        block = jnp.concatenate([block, jnp.zeros((qb, width - kw), F32)], axis=1)
    rows = qb
    while rows > 8:
        rows //= 2
        block = block[:rows] + pltpu.roll(block[rows:], width - rows, 1)
    sub = lax.broadcasted_iota(jnp.int32, (8, width), 0)
    for bit in range(3):
        block = jnp.where((sub >> bit) & 1 == 1, pltpu.roll(block, width - (1 << bit), 1), block)
    return jnp.sum(block, axis=0, keepdims=True)


def norm_kernel(order_ref, x_ref, gain_ref, shift_ref, out_ref, turned_ref, scratch):
    shards = order_ref.shape[0]
    part = scratch.shape[0] // shards
    field = x_ref[0].astype(F32)
    centre = field - jnp.mean(field, axis=-1, keepdims=True)
    spread = jnp.mean(centre * centre, axis=-1, keepdims=True)
    normed = (centre * lax.rsqrt(spread + EPS) * gain_ref[...] + shift_ref[...]).astype(BF16)
    out_ref[0] = normed
    scratch[...] = normed.T
    for t in range(shards):
        source = pl.ds(pl.multiple_of(order_ref[t] * part, part), part)
        turned_ref[0, t * part : (t + 1) * part] = scratch[source, :]


def norm_block(order, x, gain, shift):
    rows, size, width = x.shape
    line = pl.BlockSpec((1, width), lambda r, o: (0, 0))
    tile = pl.BlockSpec((1, size, width), lambda r, o: (r, 0, 0))
    normed, turned = pl.pallas_call(
        norm_kernel,
        grid_spec=pltpu.PrefetchScalarGridSpec(
            num_scalar_prefetch=1,
            grid=(rows,),
            in_specs=[tile, line, line],
            out_specs=[tile, pl.BlockSpec((1, width, size), lambda r, o: (r, 0, 0))],
            scratch_shapes=[pltpu.VMEM((width, size), BF16)],
        ),
        out_shape=[
            jax.ShapeDtypeStruct((rows, size, width), BF16),
            jax.ShapeDtypeStruct((rows, width, size), BF16),
        ],
        compiler_params=params(),
        cost_estimate=cost(10 * rows * size * width, rows * size * width * 6),
        name="norm_block",
    )(order, x, gain, shift)
    return normed.reshape(rows * size, width), turned


def proj_kernel(scaled, x_ref, w_ref, o_ref):
    out = dot_nn(x_ref[...], w_ref[...]).astype(BF16)
    o_ref[...] = jnp.where(pl.program_id(0) < scaled, out * 0.125, out) if scaled else out


def project(x, w, first, cols, scaled, bn=1024):
    tokens, model = x.shape
    return pl.pallas_call(
        functools.partial(proj_kernel, scaled // bn),
        grid=(cols // bn,),
        in_specs=[
            pl.BlockSpec((tokens, model), lambda n: (0, 0), pipeline_mode=pl.Buffered(1)),
            pl.BlockSpec((model, bn), lambda n: (0, n + first // bn)),
        ],
        out_specs=pl.BlockSpec((tokens, bn), lambda n: (0, n)),
        out_shape=jax.ShapeDtypeStruct((tokens, cols), BF16),
        compiler_params=params(),
        cost_estimate=cost(2 * tokens * model * cols, 2 * (tokens * model + model * cols + tokens * cols)),
        name="project",
    )(x, w)


def split_pair(field, even):
    zero = jnp.zeros_like(field)
    return jnp.concatenate([jnp.where(even, field, zero), jnp.where(even, zero, field)], axis=0)


def join_pair(field, even):
    half = field.shape[0] // 2
    return jnp.where(even, field[:half], field[half:])


def attn_fwd_kernel(qb, n, q_ref, *refs):
    bias_ref, mask_ref, o_ref, inv_ref, e_ref = refs[2 * n :]
    blocks = q_ref.shape[0] // qb
    kw = bias_ref.shape[-1]
    even = lax.broadcasted_iota(jnp.int32, (qb, 128), 1) < 64

    @pl.loop(0, q_ref.shape[1] // 128)
    def _(pair):
        cols = pl.ds(pl.multiple_of(pair * 128, 128), 128)
        k = jnp.concatenate([r[:, cols] for r in refs[:n]], axis=0)
        v = jnp.concatenate([r[:, cols] for r in refs[n : 2 * n]], axis=0)
        raw = [
            dot_nt(split_pair(q_ref[b * qb : (b + 1) * qb, cols], even), k[b * qb : b * qb + kw]) for b in range(blocks)
        ]
        for b, scores in enumerate(raw):
            rows = slice(b * qb, (b + 1) * qb)
            keys = slice(b * qb, b * qb + kw)
            mask = mask_ref[0, b]
            scores = jnp.concatenate(
                [scores[:qb] + (bias_ref[2 * pair] + mask), scores[qb:] + (bias_ref[2 * pair + 1] + mask)], axis=0
            )
            peak = jnp.max(scores, axis=-1, keepdims=True)
            expo = jnp.exp(scores - peak)
            inv = 1.0 / jnp.sum(expo, axis=-1, keepdims=True)
            expo = expo.astype(BF16)
            e_ref[0, pair, b] = expo
            inv = join_pair(jnp.broadcast_to(inv, (2 * qb, 128)), even)
            mixed = join_pair(dot_nn(expo, v[keys]), even)
            inv_ref[rows, cols] = inv
            o_ref[rows, cols] = (mixed * inv).astype(BF16)


def key_specs(n, size, cols, model, begin):
    def at(first):
        return pl.BlockSpec((size, cols), lambda r: (r, (first + begin) // cols))

    return [*[at(0)] * (n - 1), at(model), *[at(model)] * (n - 1), at(2 * model)]


def attn_fwd(kvs, bias, mask):
    heads, qb, kw = bias.shape
    pairs = heads // 2
    model = heads * 64
    rows, blocks = mask.shape[:2]
    size = blocks * qb
    n = len(kvs)
    cells = rows * blocks * heads * qb * kw
    tile = pl.BlockSpec((size, model), lambda r: (r, 0))
    return pl.pallas_call(
        functools.partial(attn_fwd_kernel, qb, n),
        grid=(rows,),
        in_specs=[
            tile,
            *key_specs(n, size, model, model, 0),
            pl.BlockSpec((heads, qb, kw), lambda r: (0, 0, 0), pipeline_mode=pl.Buffered(1)),
            pl.BlockSpec((1, blocks, qb, kw), lambda r: (r, 0, 0, 0)),
        ],
        out_specs=[
            tile,
            tile,
            pl.BlockSpec((1, pairs, blocks, 2 * qb, kw), lambda r: (r, 0, 0, 0, 0)),
        ],
        out_shape=[
            jax.ShapeDtypeStruct((rows * size, model), BF16),
            jax.ShapeDtypeStruct((rows * size, model), F32),
            jax.ShapeDtypeStruct((rows, pairs, blocks, 2 * qb, kw), BF16),
        ],
        compiler_params=params(),
        cost_estimate=cost(cells * 256, cells * 4),
        name="attn_fwd",
    )(kvs[-1], *kvs, *kvs, bias, mask)


def attn_bwd_kernel(qb, width, n, q_ref, *refs):
    e_ref, inv_ref, o_ref, g_ref = refs[2 * n : 2 * n + 4]
    dq_ref, dk_ref, dv_ref, diag_ref, sums, dk_acc, dv_acc = refs[-7:]
    blocks = q_ref.shape[0] // qb
    kw = e_ref.shape[-1]
    row = pl.program_id(0)
    even = lax.broadcasted_iota(jnp.int32, (qb, 128), 1) < 64

    @pl.when(row == 0)
    def _():
        sums[...] = jnp.zeros_like(sums)

    @pl.loop(0, q_ref.shape[1] // 128)
    def _(pair):
        cols = pl.ds(pl.multiple_of(pair * 128, 128), 128)
        k = jnp.concatenate([r[:, cols] for r in refs[:n]], axis=0)
        v = jnp.concatenate([r[:, cols] for r in refs[n : 2 * n]], axis=0)
        dk_acc[...] = jnp.zeros_like(dk_acc)
        dv_acc[...] = jnp.zeros_like(dv_acc)
        for b in range(blocks):
            rows = slice(b * qb, (b + 1) * qb)
            keys = slice(b * qb, b * qb + kw)
            grad = (g_ref[rows, cols].astype(F32) * inv_ref[rows, cols]).astype(BF16)
            weigh = grad.astype(F32) * o_ref[rows, cols].astype(F32)
            delta = jnp.sum(split_pair(weigh, even), axis=-1, keepdims=True)
            grad = split_pair(grad, even)
            expo = e_ref[0, pair, b]
            dscore = expo.astype(F32) * (dot_nt(grad, v[keys]) - delta)
            sums[pair] += dscore
            dscore = dscore.astype(BF16)
            dq_ref[rows, cols] = (join_pair(dot_nn(dscore, k[keys]), even) * 0.125).astype(BF16)
            dk_acc[:, keys] += dot_tn(split_pair(q_ref[rows, cols], even), dscore)
            dv_acc[:, keys] += dot_tn(grad, expo)
        dk_ref[0, cols, :] = dk_acc[...].astype(BF16)
        dv_ref[0, cols, :] = dv_acc[...].astype(BF16)

        @pl.when(row == pl.num_programs(0) - 1)
        def _():
            diag_ref[pair, 0:1] = diagonal_sums(sums[pair, :qb], width)
            diag_ref[pair, 1:2] = diagonal_sums(sums[pair, qb:], width)


def attn_bwd(kvs, e, inv, o, g, width, begin, end, grads=()):
    rows, pairs, blocks, qb2, kw = e.shape
    qb = qb2 // 2
    size = blocks * qb
    n = len(kvs)
    window = n * size
    model = o.shape[1]
    count = end - begin
    cols = count * 128
    at = begin // count
    share = e.size * count // pairs
    tile = pl.BlockSpec((size, cols), lambda r: (r, at))
    side = pl.BlockSpec((1, cols, window), lambda r: (r, at, 0))
    return pl.pallas_call(
        functools.partial(attn_bwd_kernel, qb, width, n),
        grid=(rows,),
        in_specs=[
            tile,
            *key_specs(n, size, cols, model, begin * 128),
            pl.BlockSpec((1, count, blocks, qb2, kw), lambda r: (r, at, 0, 0, 0)),
            *[tile] * 3,
            *[pl.BlockSpec(memory_space=pl.ANY)] * len(grads),
        ],
        out_specs=[tile, side, side, pl.BlockSpec((count, 8, width), lambda r: (at, 0, 0))],
        out_shape=[
            jax.ShapeDtypeStruct(o.shape, BF16),
            jax.ShapeDtypeStruct((rows, model, window), BF16),
            jax.ShapeDtypeStruct((rows, model, window), BF16),
            jax.ShapeDtypeStruct((pairs, 8, width), F32),
        ],
        scratch_shapes=[pltpu.VMEM((count, qb2, kw), F32)] + [pltpu.VMEM((128, window), F32)] * 2,
        input_output_aliases={1 + 2 * n + 4 + i: i for i in range(len(grads))},
        compiler_params=params(),
        cost_estimate=cost(share * 512, share * 4),
        name="attn_bwd",
    )(kvs[-1], *kvs, *kvs, e, inv, o, g, *grads)


def middle_kernel(order_ref, a_ref, w_ref, x_ref, gain_ref, shift_ref, mid_ref, norm_ref, turned_ref, mixed_ref, scratch):
    shards = order_ref.shape[0]
    part = scratch.shape[0] // shards

    def turn(field, out_ref):
        scratch[...] = field.T
        for t in range(shards):
            out_ref[t * part : (t + 1) * part] = scratch[pl.ds(pl.multiple_of(order_ref[t] * part, part), part), :]

    middle = x_ref[...].astype(F32) + dot_nn(a_ref[...], w_ref[...])
    mid_ref[...] = middle
    centre = middle - jnp.mean(middle, axis=-1, keepdims=True)
    spread = jnp.mean(centre * centre, axis=-1, keepdims=True)
    normed = (centre * lax.rsqrt(spread + EPS) * gain_ref[...] + shift_ref[...]).astype(BF16)
    norm_ref[...] = normed
    turn(normed, turned_ref)
    turn(a_ref[...], mixed_ref)


def middle_block(order, attended, w_attn, x, gain, shift, bm):
    tokens, model = x.shape
    tile = pl.BlockSpec((bm, model), lambda i, o: (i, 0))
    turned = pl.BlockSpec((model, bm), lambda i, o: (0, i))
    line = pl.BlockSpec((1, model), lambda i, o: (0, 0))
    return pl.pallas_call(
        middle_kernel,
        grid_spec=pltpu.PrefetchScalarGridSpec(
            num_scalar_prefetch=1,
            grid=(tokens // bm,),
            in_specs=[tile, pl.BlockSpec((model, model), lambda i, o: (0, w_attn.shape[1] // model - 1)), tile, line, line],
            out_specs=[tile, tile, turned, turned],
            scratch_shapes=[pltpu.VMEM((model, bm), BF16)],
        ),
        out_shape=[
            jax.ShapeDtypeStruct((tokens, model), F32),
            jax.ShapeDtypeStruct((tokens, model), BF16),
            jax.ShapeDtypeStruct((model, tokens), BF16),
            jax.ShapeDtypeStruct((model, tokens), BF16),
        ],
        compiler_params=params(),
        cost_estimate=cost(2 * tokens * model * model, tokens * model * 14 + model * model * 2),
        name="middle_block",
    )(order, attended, w_attn, x, gain, shift)


def ffn_kernel(
    bm, first, last, chip_ref, n2_ref, n2t_ref, cot_ref, acc_ref, gin_ref, wu_ref, bu_ref, d0_ref, d1_ref, bd_ref, *refs
):
    out_ref, gn_ref, us_ref, uk_ref, ds_ref, dk_ref, gbu_ref, sums, wd, act_s, gpre_s, spare = refs[-12:]
    step = pl.program_id(0)
    tokens = n2_ref.shape[0]
    part = d0_ref.shape[0] // 2
    core = chip_ref[chip_ref.shape[0] - 1]

    @pl.when(step == 0)
    def _():
        if first:
            sums[...] = acc_ref[...] + bd_ref[...]
            gn_ref[...] = jnp.zeros_like(gn_ref)
        else:
            sums[...] = acc_ref[...]
            gn_ref[...] = gin_ref[...]

    for c in range(2):
        for i, d_ref in enumerate((d0_ref, d1_ref)):
            wd[(2 * c + i) * part : (2 * c + i + 1) * part] = d_ref[c * part : (c + 1) * part]
    gbu_ref[...] = jnp.zeros_like(gbu_ref)

    def tile(rows):
        act, slope = gelu_parts(dot_nn(n2_ref[rows, :], wu_ref[...]) + bu_ref[...])
        gpre = (dot_nt(cot_ref[rows, :], wd[...]) * slope).astype(BF16)
        act = act.astype(BF16)
        act_s[rows, :] = act
        gpre_s[rows, :] = gpre
        gbu_ref[...] += jnp.sum(gpre.astype(F32), axis=0, keepdims=True)
        sums[rows, :] += dot_nn(act, wd[...])
        gn_ref[rows, :] += dot_nt(gpre, wu_ref[...])

    for i in range(tokens // bm):
        tile(slice(i * bm, (i + 1) * bm))

    spare[...] = dot_tn(act_s[...], cot_ref[...]).astype(BF16).reshape(spare.shape)
    ds_ref[0] = spare[1 - core]
    dk_ref[0] = spare[core]
    half = n2t_ref.shape[0] // 2
    us_ref[...] = dot_nn(n2t_ref[:half], gpre_s[...]).astype(BF16).reshape(us_ref.shape)
    uk_ref[...] = dot_nn(n2t_ref[half:], gpre_s[...]).astype(BF16).reshape(uk_ref.shape)

    @pl.when(step == pl.num_programs(0) - 1)
    def _():
        out_ref[...] = sums[...].astype(out_ref.dtype)


def ffn_block(chips, n2, n2t, cot, acc, gin, w, b_up, b_down, begin, end, first, last, bm, grads=()):
    tokens, model = n2.shape
    pairs = chips.shape[0] - 1
    shards = 2 * pairs
    part = model // shards
    hidden = b_up.shape[1]
    fc = hidden // pairs
    once = pl.Buffered(1)
    whole = pl.BlockSpec((tokens, model), lambda j, o: (0, 0), pipeline_mode=once)
    by_col = pl.BlockSpec((pairs, part, fc), lambda j, o: (0, 0, o[j + begin]))
    by_row = pl.BlockSpec((1, fc // 2, model), lambda j, o: (j + begin, 0, 0))
    return pl.pallas_call(
        functools.partial(ffn_kernel, bm, first, last),
        grid_spec=pltpu.PrefetchScalarGridSpec(
            num_scalar_prefetch=1,
            grid=(end - begin,),
            in_specs=[
                whole,
                pl.BlockSpec((model, tokens), lambda j, o: (0, 0), pipeline_mode=once),
                whole,
                whole,
                pl.BlockSpec((8, model), lambda j, o: (0, 0)) if first else whole,
                pl.BlockSpec((model, fc), lambda j, o: (0, o[j + begin])),
                pl.BlockSpec((1, fc), lambda j, o: (0, o[j + begin])),
                pl.BlockSpec((2 * part, model), lambda j, o: (o[j + begin], hidden // model)),
                pl.BlockSpec((2 * part, model), lambda j, o: (o[j + begin], hidden // model + 1)),
                pl.BlockSpec((1, model), lambda j, o: (0, 0)),
                *[pl.BlockSpec(memory_space=pl.ANY)] * len(grads),
            ],
            out_specs=[
                pl.BlockSpec((tokens, model), lambda j, o: (0, 0)),
                pl.BlockSpec((tokens, model), lambda j, o: (0, 0)),
                by_col,
                by_col,
                by_row,
                by_row,
                pl.BlockSpec((1, fc), lambda j, o: (0, o[j + begin])),
            ],
            scratch_shapes=[
                pltpu.VMEM((tokens, model), F32),
                pltpu.VMEM((fc, model), BF16),
                pltpu.VMEM((tokens, fc), BF16),
                pltpu.VMEM((tokens, fc), BF16),
                pltpu.VMEM((2, fc // 2, model), BF16),
            ],
        ),
        out_shape=[
            jax.ShapeDtypeStruct((tokens, model), BF16 if last else F32),
            jax.ShapeDtypeStruct((tokens, model), F32),
            jax.ShapeDtypeStruct((pairs, part, hidden), BF16),
            jax.ShapeDtypeStruct((pairs, part, hidden), BF16),
            jax.ShapeDtypeStruct((pairs, fc // 2, model), BF16),
            jax.ShapeDtypeStruct((pairs, fc // 2, model), BF16),
            jax.ShapeDtypeStruct((1, hidden), F32),
        ],
        input_output_aliases={11 + i: 2 + i for i in range(len(grads))},
        compiler_params=params(),
        cost_estimate=cost(
            12 * tokens * model * fc * (end - begin),
            tokens * model * 20 + model * fc * (end - begin) * 8,
        ),
        name="ffn_block",
    )(chips, n2, n2t, cot, acc, gin, w, b_up, w, w, b_down, *grads)


def standard(field):
    centre = field - jnp.mean(field, axis=-1, keepdims=True)
    rate = lax.rsqrt(jnp.mean(centre * centre, axis=-1, keepdims=True) + EPS)
    return centre * rate, rate


def norm_back(field, gain, e):
    n, rate = standard(field)
    eg = e * gain
    grad = rate * (eg - jnp.mean(eg, axis=-1, keepdims=True) - n * jnp.mean(eg * n, axis=-1, keepdims=True))
    return grad, n


def middle_back_kernel(gn_ref, mid_ref, cot_ref, w_ref, gain_ref, gm_ref, gb_ref, ga_ref, gg_ref, gs_ref):
    @pl.when(pl.program_id(0) == 0)
    def _():
        gg_ref[...] = jnp.zeros_like(gg_ref)
        gs_ref[...] = jnp.zeros_like(gs_ref)

    e = gn_ref[...]
    grad, n = norm_back(mid_ref[...], gain_ref[...], e)
    gg_ref[...] += jnp.sum(e * n, axis=0, keepdims=True)
    gs_ref[...] += jnp.sum(e, axis=0, keepdims=True)
    grad = cot_ref[...].astype(F32) + grad
    gm_ref[...] = grad
    branch = grad.astype(BF16)
    gb_ref[...] = branch
    ga_ref[...] = dot_nt(branch, w_ref[...]).astype(BF16)


def middle_back(gn2, middle, cot, w_attn, gain, bm):
    tokens, model = middle.shape
    tile = pl.BlockSpec((bm, model), lambda i: (i, 0))
    line = pl.BlockSpec((1, model), lambda i: (0, 0))
    return pl.pallas_call(
        middle_back_kernel,
        grid=(tokens // bm,),
        in_specs=[tile, tile, tile, pl.BlockSpec((model, model), lambda i: (0, w_attn.shape[1] // model - 1)), line],
        out_specs=[tile, tile, tile, line, line],
        out_shape=[
            jax.ShapeDtypeStruct((tokens, model), F32),
            jax.ShapeDtypeStruct((tokens, model), BF16),
            jax.ShapeDtypeStruct((tokens, model), BF16),
            jax.ShapeDtypeStruct((1, model), F32),
            jax.ShapeDtypeStruct((1, model), F32),
        ],
        compiler_params=params(),
        cost_estimate=cost(2 * tokens * model * model, tokens * model * 18 + model * model * 2),
        name="middle_back",
    )(gn2, middle, cot, w_attn, gain)


def attn_weights_kernel(n, *refs):
    turned = refs[:n]
    at_ref, dq_ref, dk_ref, dv_ref, gb_ref, small_ref = refs[n : n + 6]
    sends, keeps = refs[n + 6 : n + 8], refs[n + 8 :]
    model = gb_ref.shape[1]
    rows, _, size = turned[0].shape
    half = sends[0].shape[0]
    part = sends[1].shape[1]

    def store(field, side, value):
        value = value.astype(BF16).reshape(half, part, model)
        for step, outs in enumerate((sends, keeps)):

            @pl.when(pl.program_id(0) == step)
            def _():
                outs[field][:, :part, side * model : (side + 1) * model] = value

    def over_window(ref):
        return sum(
            dot_nt(turned[b][r], ref[r, :, b * size : (b + 1) * size]) for r in range(rows) for b in range(n)
        )

    for step, outs in enumerate((sends, keeps)):

        @pl.when(pl.program_id(0) == step)
        def _():
            outs[0][:, part:, :] = small_ref[...]

    store(0, 0, sum(dot_nn(turned[-1][r], dq_ref[r]) for r in range(rows)))
    store(0, 1, over_window(dk_ref))
    store(1, 0, over_window(dv_ref))
    store(1, 1, dot_nn(at_ref[...], gb_ref[...]))


def attn_weights(turned, mixed, dq, dk, dv, branch, small, shards):
    rows, model, size = turned[0].shape
    tokens = branch.shape[0]
    n = len(turned)
    window = n * size
    half = shards // 2
    part = model // shards

    def full(*shape):
        return pl.BlockSpec(shape, lambda i: (0,) * len(shape), pipeline_mode=pl.Buffered(1))

    large = n * rows > 32
    buffers = pl.Buffered(1 if large else 2)
    shapes = [(half, part + small.shape[1], 2 * model), (half, part, 2 * model)] * 2
    return pl.pallas_call(
        functools.partial(attn_weights_kernel, n),
        grid=(2,),
        in_specs=[
            *[pl.BlockSpec((rows, model // 2, size), lambda i: (0, i, 0), pipeline_mode=buffers)] * n,
            pl.BlockSpec((model // 2, tokens), lambda i: (i, 0), pipeline_mode=buffers),
            full(rows, size, model),
            full(rows, model, window),
            full(rows, model, window),
            full(tokens, model),
            pl.BlockSpec((half, *small.shape[1:]), lambda i: (i, 0, 0)),
        ],
        out_specs=[pl.BlockSpec(shape, lambda i: (0, 0, 0)) for shape in shapes],
        out_shape=[jax.ShapeDtypeStruct(shape, BF16) for shape in shapes],
        compiler_params=params(60 if large else 56),
        cost_estimate=cost(4 * model * model * (tokens + rows * window), 8 * rows * model * window + 16 * model * model, LIGHT),
        name="attn_weights",
    )(*turned, mixed, dq.reshape(rows, size, model), dk, dv, branch, small)


def norm_grad_kernel(n, dq_ref, dk_ref, dv_ref, w_ref, *refs):
    model = w_ref.shape[0]
    near, far, (own_ref, gg_ref, gs_ref) = refs[:n], refs[n : 2 * n - 1], refs[2 * n - 1 :]
    size = own_ref.shape[1]

    @pl.when(pl.program_id(0) == 0)
    def _():
        gg_ref[...] = jnp.zeros_like(gg_ref)
        gs_ref[...] = jnp.zeros_like(gs_ref)

    for b in range(n):
        side = slice(b * size, (b + 1) * size)
        grad = dot_nn(w_ref[:, model : 2 * model], dk_ref[0, :, side])
        grad = (grad + dot_nn(w_ref[:, 2 * model :], dv_ref[0, :, side])).T
        if b == n - 1:
            grad += dot_nt(dq_ref[0], w_ref[:, :model])
            own_ref[0] = grad
        else:
            far[b][0] = grad.astype(BF16)
        normed, _ = standard(near[b][0].astype(F32))
        gg_ref[...] += jnp.sum(grad * normed, axis=0, keepdims=True)
        gs_ref[...] += jnp.sum(grad, axis=0, keepdims=True)


def norm_grad(dq, dk, dv, w_attn, near):
    rows, model, window = dk.shape
    n = len(near)
    size = window // n
    tile = pl.BlockSpec((1, size, model), lambda r: (r, 0, 0))
    line = pl.BlockSpec((1, model), lambda r: (0, 0))
    side = pl.BlockSpec((1, model, window), lambda r: (r, 0, 0))
    shape = (rows, size, model)
    return pl.pallas_call(
        functools.partial(norm_grad_kernel, n),
        grid=(rows,),
        in_specs=[
            tile,
            side,
            side,
            pl.BlockSpec((model, 3 * model), lambda r: (0, 0), pipeline_mode=pl.Buffered(1)),
            *[tile] * n,
        ],
        out_specs=[*[tile] * n, line, line],
        out_shape=[
            *[jax.ShapeDtypeStruct(shape, BF16)] * (n - 1),
            jax.ShapeDtypeStruct(shape, F32),
            jax.ShapeDtypeStruct((1, model), F32),
            jax.ShapeDtypeStruct((1, model), F32),
        ],
        compiler_params=params(),
        cost_estimate=cost(2 * rows * model * model * (size + 2 * window), rows * model * window * 8 + 6 * model * model),
        name="norm_grad",
    )(dq.reshape(shape), dk, dv, w_attn, *[x.reshape(shape) for x in near])


def first_back_kernel(dn_ref, back_ref, x_ref, gm_ref, gain_ref, out_ref):
    e = dn_ref[...] + back_ref[...].astype(F32)
    grad, _ = norm_back(x_ref[...].astype(F32), gain_ref[...], e)
    out_ref[...] = (gm_ref[...] + grad).astype(BF16)


def first_back(dn, back, x, gm, gain, bm):
    tokens, model = x.shape
    tile = pl.BlockSpec((bm, model), lambda i: (i, 0))
    return pl.pallas_call(
        first_back_kernel,
        grid=(tokens // bm,),
        in_specs=[tile, tile, tile, tile, pl.BlockSpec((1, model), lambda i: (0, 0))],
        out_specs=tile,
        out_shape=jax.ShapeDtypeStruct((tokens, model), BF16),
        compiler_params=params(),
        cost_estimate=cost(20 * tokens * model, tokens * model * 14, 0.0),
        name="first_back",
    )(dn, back, x, gm, gain)


def flip(axis, count, bit):
    return functools.partial(lax.ppermute, axis_name=axis, perm=[(i, i ^ bit) for i in range(count)])


def add_low(a, b):
    return (a.astype(F32) + b.astype(F32)).astype(BF16)


def merge_kernel(n, *refs):
    ins, outs = refs[: 2 * n], refs[2 * n :]
    for i, out in enumerate(outs):
        out[...] = (ins[2 * i][...].astype(F32) + ins[2 * i + 1][...].astype(F32)).astype(out.dtype)


def merge(pairs, backwards, final):
    ins, in_specs, out_shape, out_specs = [], [], [], []
    count = pairs[0][0].shape[0]
    half = max(count // 2, 1)
    tiles = 2
    for (a, b), back in zip(pairs, backwards):
        _, rows, cols = a.shape
        shape = (1, rows // tiles, cols)
        if final:
            picks = [lambda q, t: (0, t, 0)]
        elif back:
            picks = [lambda q, t: (q, t, 0), lambda q, t: (q + half, t, 0)]
        else:
            picks = [lambda q, t: (2 * q, t, 0), lambda q, t: (2 * q + 1, t, 0)]
        for pick in picks:
            ins += [a, b]
            in_specs += [pl.BlockSpec(shape, pick)] * 2
            out_specs.append(pl.BlockSpec(shape, lambda q, t: (q, t, 0)))
            out_shape.append(jax.ShapeDtypeStruct((half, rows, cols), BF16))
    size = sum(a.size for a, _ in pairs)
    outs = pl.pallas_call(
        functools.partial(merge_kernel, len(out_shape)),
        grid=(half, tiles),
        in_specs=in_specs,
        out_specs=out_specs,
        out_shape=out_shape,
        compiler_params=params(),
        cost_estimate=cost(size, size * 6, LIGHT),
        name="merge",
    )(*ins)
    return list(outs) if final else list(zip(outs[0::2], outs[1::2]))


class ShardSum:
    def __init__(self, sends, keeps, shards):
        self.shards = shards
        self.bits = list(range(1, shards.bit_length() - 1))
        self.stage = 0
        self.back = [i % 2 == 1 for i in range(len(keeps))]
        self.flying = [(k, flip("fsdp", shards, 1)(s)) for k, s in zip(keeps, sends)]

    def land(self):
        return merge(self.flying, self.back, self.stage == len(self.bits))

    def launch(self, landed):
        self.flying = []
        for back, (kept, sent) in zip(self.back, landed):
            bit = (self.bits[::-1] if back else self.bits)[self.stage]
            self.flying.append((kept, flip("fsdp", self.shards, 1 << bit)(sent)))
        self.stage += 1

    def step(self, *others):
        landed, others = lax.optimization_barrier((self.land(), others))
        self.launch(landed)
        return others if len(others) != 1 else others[0]

    def finish(self):
        while self.stage < len(self.bits):
            self.launch(self.land())
        return [f[0] for f in self.land()]


def add_everywhere(field, axes):
    for axis, count in axes:
        bit = 1
        while bit < count:
            field = field + flip(axis, count, bit)(field)
            bit *= 2
    return field


def per_device(
    inputs,
    segment_ids,
    buckets,
    ln1_gain,
    ln1_bias,
    w_query,
    w_key,
    w_value,
    w_out,
    rel_bias,
    second_norm_gain,
    ln2_bias,
    w_up,
    b_up,
    w_down,
    b_down,
    cotangent,
):
    num_micro, num_rows, size, model = inputs.shape
    rows = num_micro * num_rows
    seq_len = segment_ids.shape[2]
    heads = rel_bias.shape[1]
    shards = lax.axis_size("fsdp")
    ranges = lax.axis_size("seq")
    num_buckets = rel_bias.shape[0] * shards
    hidden = w_up.shape[1]
    tokens = rows * size
    hops = min(-(-(CLIP - 1) // size), ranges - 1)
    halo = hops * size
    window = halo + size
    qb = min(128, size)
    blocks = size // qb
    kw = halo + qb
    width = -(-(kw + qb) // 128) * 128
    tile = min(256, tokens)

    me = lax.axis_index("fsdp")
    order = me ^ jnp.array([*range(1, shards, 2), *range(0, shards, 2)], jnp.int32)
    chips = jnp.append((me // 2) ^ jnp.arange(shards // 2, dtype=jnp.int32), me % 2)

    gather = functools.partial(lax.all_gather, axis_name="fsdp", axis=0, tiled=True)
    w_local = jnp.concatenate([w_query, w_key, w_value], axis=1)
    x = inputs.reshape(rows, size, model)
    w_local, x, w_out, w_up, w_down = lax.optimization_barrier((w_local, x, w_out, w_up, w_down))
    w_attn = gather(w_local)
    up = [(i, i + 1) for i in range(ranges - 1)]
    near = [x]
    if hops:
        near.insert(0, lax.ppermute(x, "seq", up))
    vectors = (ln1_gain, ln1_bias, second_norm_gain, ln2_bias, b_up, b_down, rel_bias.reshape(-1))
    packed = jnp.concatenate(vectors)[None].astype(F32)
    packed = jnp.where(jnp.arange(shards)[:, None] == me, packed, 0.0)
    packed = add_everywhere(packed, (("fsdp", shards),))
    parts, at = [], 0
    for v in vectors:
        parts.append(packed[:, at : at + v.size].reshape(1, -1))
        at += v.size
    gain1, shift1, gain2, shift2, bias_up, bias_down = parts[:6]
    table = parts[6].reshape(num_buckets, heads).astype(BF16)
    fine = hidden // shards // 2
    columns = w_up.reshape(w_up.shape[0], shards, 2, fine)
    w_ff = []
    for side in range(2):
        pieces = [columns[:, :, side].reshape(w_up.shape[0], -1)]
        down = w_down[side * fine : (side + 1) * fine].reshape(-1, w_up.shape[0], model)
        pieces += [down[i] for i in range(down.shape[0])]
        if side == 0:
            pieces.append(w_out)
        w_ff.append(gather(jnp.concatenate(pieces, axis=1)))

    place = lax.axis_index("seq") * size
    column = jnp.arange(width, dtype=jnp.int32)
    gap = halo - column
    inside = (gap >= 0) & (column > 0)
    bucket_of = jnp.where(inside, jnp.flip(jnp.pad(buckets[: halo + 1], (width - halo - 1, 0))), -1)
    onehot = bucket_of[:, None] == jnp.arange(num_buckets, dtype=jnp.int32)[None]
    by_gap = dot_nn(onehot.astype(BF16), table) + jnp.where(inside, 0.0, NEG)[:, None]
    bias = make_bias(by_gap.T, qb, kw)
    segs = segment_ids.reshape(rows, seq_len)
    segs = lax.dynamic_slice_in_dim(jnp.pad(segs, ((0, 0), (halo, 0)), constant_values=-1), place, window, 1)
    mask = jnp.stack(
        [
            jnp.where(
                segs[:, halo + b * qb : halo + (b + 1) * qb, None] == segs[:, None, b * qb : b * qb + kw], 0.0, NEG
            )
            for b in range(blocks)
        ],
        axis=1,
    ).astype(F32)

    for hop in range(hops - 1):
        moved = near[0]
        if hop == 0:
            moved, bias, mask, gain1 = lax.optimization_barrier((moved, bias, mask, gain1))
        near.insert(0, lax.ppermute(moved, "seq", up))

    normed, turned, kvs = [None] * (hops + 1), [None] * (hops + 1), [None] * (hops + 1)
    for b in range(hops, -1, -1):
        if b == hops - 2:
            near[: b + 1], kvs[b + 1 :] = lax.optimization_barrier((near[: b + 1], kvs[b + 1 :]))
        normed[b], turned[b] = norm_block(order, near[b], gain1, shift1)
        first, cols, scaled = (0, 3 * model, model) if b == hops else (model, 2 * model, 0)
        kvs[b] = project(normed[b], w_attn, first, cols, scaled)
    attended, inv, expo = attn_fwd(kvs, bias, mask)
    x = x.reshape(tokens, model)
    middle, normed_two, two_turned, mixed_turned = middle_block(order, attended, w_ff[0], x, gain2, shift2, tile)

    cot = cotangent.reshape(tokens, model)
    bias_up = bias_up.reshape(shards, 2, fine)
    tile_ff = tokens // 2 if tokens % 32 == 0 else tokens
    pairs = shards // 2
    ffn = functools.partial(ffn_block, chips, normed_two, two_turned, cot, b_down=bias_down, bm=tile_ff)
    bias_a, bias_b = (bias_up[:, side].reshape(1, -1) for side in range(2))
    part_out, part_grad, us, uk, ds, dk, grad_b_a = ffn(
        middle, jnp.zeros((8, model), F32), w_ff[0], bias_a, begin=0, end=pairs, first=True, last=False
    )
    sum_a = ShardSum([us, ds], [uk, dk], shards)
    outputs, grad_norm2, us, uk, ds, dk, grad_b_b = ffn(
        part_out, part_grad, w_ff[1], bias_b, begin=0, end=pairs, first=False, last=True
    )
    sum_b = ShardSum([us, ds], [uk, dk], shards)
    grad_b_up = jnp.stack([grad_b_a.reshape(shards, fine), grad_b_b.reshape(shards, fine)], axis=1)
    grad_b_down = jnp.sum(cot.astype(F32), axis=0, keepdims=True)

    def total(fields):
        return lax.psum(tuple(fields), "seq")

    grad_norm2 = sum_a.step(grad_norm2)
    grad_middle, grad_branch, grad_attended, grad_gain2, grad_shift2 = middle_back(
        grad_norm2, middle, cot, w_ff[0], gain2, tile
    )
    backward = functools.partial(attn_bwd, kvs, expo, inv, attended)
    half = heads // 4
    grads = backward(grad_attended, width, 0, half)
    if sum_a.stage < len(sum_a.bits):
        grad_attended, grads, sum_b.flying = sum_a.step(grad_attended, grads, sum_b.flying)
    landed, sum_a.flying = lax.optimization_barrier((sum_b.land(), sum_a.flying))
    sum_b.launch(landed)
    done_a, grad_attended, grads = lax.optimization_barrier((sum_a.finish(), grad_attended, grads))
    grads = backward(grad_attended, width, half, heads // 2, grads)
    if sum_b.stage < len(sum_b.bits):
        grads = sum_b.step(grads)
    total_a = total(done_a)
    grad_q, grad_k, grad_v, diagonal = grads
    back = None
    down = [(i + 1, i) for i in range(ranges - 1)]
    up_b, down_b = sum_b.finish()
    total_b = jnp.concatenate([*jnp.split(up_b, up_b.shape[1] // model, axis=1), down_b], axis=0)
    total_b = lax.psum_scatter(total_b, "seq", scatter_dimension=0, tiled=True)
    total_b = lax.all_gather(total_b, "seq", axis=0, tiled=True)
    *far, grad_own, grad_gain1, grad_shift1 = norm_grad(grad_q, grad_k, grad_v, w_attn, near)
    if hops:
        back = lax.ppermute(far[0], "seq", down)
    diagonal = diagonal[:, :2].reshape(heads, width)
    grad_table = lax.dot_general(onehot.astype(F32), diagonal, (((0,), (1,)), ((), ())), precision=HIGHEST)
    small = (grad_gain1, grad_shift1, grad_gain2, grad_shift2, grad_b_up, grad_b_down, grad_table)
    small = jnp.concatenate([f.reshape(shards, -1) for f in small], axis=1).astype(BF16)
    small_cols = -(-small.shape[1] // (2 * model)) * 2 * model
    small = jnp.pad(small, ((0, 0), (0, small_cols - small.shape[1]))).reshape(shards, -1, 2 * model)
    small = jnp.pad(small, ((0, 0), (0, 16 - small.shape[1]), (0, 0)))
    small = jnp.take(small, order, axis=0)
    grad_q, grad_own = lax.optimization_barrier((grad_q, grad_own))
    first_send, last_send, first_keep, last_keep = attn_weights(
        turned, mixed_turned, grad_q, grad_k, grad_v, grad_branch, small, shards
    )
    for hop in range(1, hops):
        pieces = [(far[hop].reshape(1, tokens, model), back.reshape(1, tokens, model))]
        back = merge(pieces, [False], True)[0].reshape(rows, size, model)
        if hop < hops - 1:
            back = lax.ppermute(back, "seq", down)
    first_send, last_send, total_a, back = lax.optimization_barrier((first_send, last_send, total_a, back))
    if hops > 1:
        back = lax.ppermute(back, "seq", down)
    sum_c = ShardSum([first_send, last_send], [first_keep, last_keep], shards)
    while sum_c.stage < len(sum_c.bits):
        sum_c.launch(sum_c.land())
    sum_c.flying, total_b = lax.optimization_barrier((sum_c.flying, total_b))
    done_c = sum_c.finish()
    total_c = total(done_c)
    (grad_own, total_b), _ = lax.optimization_barrier(((grad_own, total_b), done_c))
    if back is None:
        back = jnp.zeros((rows, size, model), BF16)
    input_grad = first_back(grad_own.reshape(tokens, model), back.reshape(tokens, model), x, grad_middle, gain1, tile)
    up_a, down_a = (f.astype(F32) for f in total_a)
    total_b = total_b.astype(F32)
    count = up_b.shape[0] * (up_b.shape[1] // model)
    up_b = jnp.concatenate(jnp.split(total_b[:count], up_b.shape[1] // model, axis=0), axis=1)
    down_b = total_b[count:]
    grad_w_up = jnp.stack([up_a.reshape(-1, shards, fine), up_b.reshape(-1, shards, fine)], axis=2).reshape(w_up.shape)
    grad_w_down = jnp.concatenate([down_a, down_b], axis=0)
    part = model // shards
    small = total_c[0][part:].astype(F32).reshape(-1)
    grad_first, grad_last = total_c[0][:part].astype(F32), total_c[1].astype(F32)
    finals, at = [], 0
    for v in vectors:
        finals.append(small[at : at + v.size].reshape(v.shape))
        at += v.size
    finals[6] = finals[6].reshape(rel_bias.shape)

    return (
        outputs.reshape(inputs.shape),
        input_grad.reshape(inputs.shape),
        finals[0],
        finals[1],
        grad_first[:, :model],
        grad_first[:, model:],
        grad_last[:, :model],
        grad_last[:, model:],
        finals[6],
        finals[2],
        finals[3],
        grad_w_up,
        finals[4],
        grad_w_down,
        finals[5],
    )


def solution(mesh):
    token = P(None, "fsdp", "seq", None)
    vector = P("fsdp")
    matrix = P("fsdp", None)
    return jax.shard_map(
        per_device,
        mesh=mesh,
        in_specs=(
            token, P(None, "fsdp", None), P(), vector, vector, matrix, matrix, matrix, matrix, matrix,
            vector, vector, matrix, vector, matrix, vector, token,
        ),
        out_specs=(
            token, token, vector, vector, matrix, matrix, matrix, matrix, matrix,
            vector, vector, matrix, vector, matrix, vector,
        ),
        check_vma=False,
    )
```
